256 devices in a mesh: ox: 16 (over y, z_lo, core), oy: 16 (over z_hi, x).
Axes of the slice: x: 4, y: 4, z: 8 (z_hi: 4, z_lo: 2; z = z_hi * 2 + z_lo), core: 2. Of those that a mesh axis runs over, the one named last changes fastest.
Arguments:
- slip_rate: bfloat16 [4, 8192], P(None, ('ox', 'oy')), may hold values from -6 to 6
- green_kernel: bfloat16 [8192, 9, 8192], P(('ox', 'oy')), may hold values from -1 to 1
- intersection: int32 [256, 9], P(('ox', 'oy')), may hold values 0 or 1
- wet_mask: int32 [4096, 8192], P('ox', 'oy'), may hold values 0 or 1
- column_height: float32 [4096, 8192], P('ox', 'oy'), may hold values from 3 to 5
- east_flow: float32 [4096, 8192], P('ox', 'oy'), may hold values from -3 to 3
- north_flow: float32 [4096, 8192], P('ox', 'oy'), may hold values from -3 to 3
Outputs:
- height_out: float32 [4096, 8192], P('ox', 'oy')
- east_out: float32 [4096, 8192], P('ox', 'oy')
- north_out: float32 [4096, 8192], P('ox', 'oy')
The draws below stay inside these ranges and needn't reach their ends.
All inputs are finite; a program needn't handle non-finite values. No bound on the sum of `intersection` or of `wet_mask` on one device may be relied on, other than what follows from the above.
Results may differ from the reference program's by a relative error of at most 0.0003.
Values sent between devices are 32-bit elements; how exact they have to be, the bound alone decides.
No kernel may reach another device: no remote copies, remote signals or barrier semaphores. Data moves between devices by JAX's collectives and lax.ppermute only.
A program may use at most 64 MiB of HBM per device.

```python
import jax
import jax.numpy as jnp
from jax import lax

F_DEV = 32
STEPS = 4
COARSE = 4
NX = 4096
NY = 8192
BLOCKS = 256
FAULTS = 8192
UX = 64
UY = 128
UP = 8192
N_OX = 16
N_OY = 16


def plant(entries, rng, low, high):
    longest = entries.shape.index(max(entries.shape))
    spots = []
    for shift in (0, 1):
        where = [jax.random.randint(jax.random.fold_in(rng, axis), (), 0, length) for axis, length in enumerate(entries.shape)]
        where[longest] = (where[longest] + shift) % entries.shape[longest]
        spots.append(tuple(where))
    return entries.at[spots[0]].set(low).at[spots[1]].set(high)


def levels(rng, shape, shards, low, top_value):
    def one(position, shards_of):
        steps = jax.random.uniform(jax.random.fold_in(jax.random.fold_in(rng, 6), position), (shards_of,), jnp.float32, low / len(shards), top_value / len(shards))
        return jnp.repeat(jnp.exp(steps), shape[position] // shards_of).reshape((-1,) + (1,) * (len(shape) - position - 1))

    factor_of = one(*shards[0])
    for cut in shards[1:]:
        factor_of = factor_of * one(*cut)
    return factor_of


def bell_draw(rng, shape, width, bound, split=(), held_as=jnp.bfloat16):
    array = jax.random.normal(rng, shape, jnp.float32) * width
    if len(split) > 0:
        array = levels(rng, shape, split, -0.22, 0.18) * array
    return jnp.clip(array, min=-bound, max=bound).astype(held_as)


def setup_inputs(seed: int = 0) -> dict:
    key_list = jax.random.split(jax.random.key(seed), 8)
    return {
        "slip_rate": bell_draw(key_list[0], (STEPS, FAULTS), 1.0, 6.0, ((1, 256),)),
        "green_kernel": bell_draw(key_list[1], (FAULTS, 9, UP), F_DEV ** -0.5, 1.0, ((0, 256),)),
        "intersection": plant((jax.random.randint(key_list[2], (BLOCKS, 9), 0, 3) < 2).astype(jnp.int32), jax.random.fold_in(key_list[2], 1), 0, 1),
        "wet_mask": plant((jax.random.randint(key_list[3], (NX, NY), 0, 10) < 9).astype(jnp.int32), jax.random.fold_in(key_list[3], 1), 0, 1),
        "column_height": jnp.clip(3.0 + 2.0 * jax.random.uniform(key_list[4], (NX, NY), jnp.float32) ** levels(key_list[4], (NX, NY), ((0, 16), (1, 16)), -0.2, 0.2), 3.0, 5.0),
        "east_flow": bell_draw(key_list[5], (NX, NY), 0.5, 3.0, ((0, 16), (1, 16)), jnp.float32),
        "north_flow": bell_draw(key_list[6], (NX, NY), 0.5, 3.0, ((0, 16), (1, 16)), jnp.float32),
    }


gravity = 1.0
ratio = 0.2
source = 0.05


def lax_friedrichs(extended):
    height = extended[0]
    east = extended[1]
    north = extended[2]
    flux_x = jnp.stack([east, east * east / height + 0.5 * gravity * height * height, east * north / height])
    flux_y = jnp.stack([north, east * north / height, north * north / height + 0.5 * gravity * height * height])
    average = 0.25 * (extended[:, 2:, 1:-1] + extended[:, :-2, 1:-1] + extended[:, 1:-1, 2:] + extended[:, 1:-1, :-2])
    average = average - 0.5 * ratio * (flux_x[:, 2:, 1:-1] - flux_x[:, :-2, 1:-1])
    return average - 0.5 * ratio * (flux_y[:, 1:-1, 2:] - flux_y[:, 1:-1, :-2])


def reference(slip_rate, green_kernel, intersection, wet_mask, column_height, east_flow, north_flow):
    slips = slip_rate.reshape(STEPS, BLOCKS, F_DEV).transpose(1, 0, 2)
    kernels = green_kernel.reshape(BLOCKS, F_DEV, 9 * UP)

    def one_block(pieces):
        slip_block, kernel_block, cover = pieces
        term = jnp.dot(slip_block, kernel_block, preferred_element_type=jnp.float32).reshape(STEPS, 9, UP)
        return term * cover.astype(jnp.float32)[None, :, None]

    partial_value = lax.map(one_block, (slips, kernels, intersection))
    partial_value = partial_value.reshape(N_OX, N_OY, STEPS, 3, 3, UX, UY)
    coarse = jnp.zeros((N_OX, N_OY, STEPS, UX, UY), jnp.float32)
    for row_off in range(3):
        for col_off in range(3):
            padded = jnp.pad(partial_value[:, :, :, row_off, col_off], ((1, 1), (1, 1), (0, 0), (0, 0), (0, 0)))
            coarse = coarse + padded[2 - row_off:2 - row_off + N_OX, 2 - col_off:2 - col_off + N_OY]
    coarse = coarse.transpose(2, 0, 3, 1, 4).reshape(STEPS, NX // COARSE, NY // COARSE)
    wet = wet_mask.astype(jnp.float32)
    state = jnp.stack([column_height, east_flow, north_flow])
    for section in range(STEPS):
        extended = jnp.pad(state, ((0, 0), (1, 1), (1, 1)), mode="edge")
        updated = lax_friedrichs(extended)
        fine = jnp.repeat(jnp.repeat(coarse[section], COARSE, axis=0), COARSE, axis=1)
        state = jnp.stack([updated[0] + source * fine, updated[1] * wet, updated[2] * wet])
    return state[0], state[1], state[2]
```

```python
import functools

import jax
import jax.numpy as jnp
from jax import lax
from jax.experimental import pallas as pl
from jax.experimental.pallas import tpu as pltpu
from jax.sharding import PartitionSpec as P

STEPS = 4
SIDE = 16
ROWS = 256
COLS = 512
LANES = 128
UX = 64
EXT = ROWS + 8
WIDE = COLS + LANES
MAIN = STEPS * UX
RING = MAIN + 8
SLIVER = 3 * MAIN
EDGE = SLIVER + 16
ROW_MSG = EDGE + 64
TURNED = RING
COL_MSG = RING + 48
VMEM_LIMIT = 48 * 1024 * 1024
UNROLL = 4


def partners(axis, parity, reach):
    return [
        (i, (i + reach if (i // reach) % 2 == parity else i - reach) % SIDE)
        for i in range(SIDE)
    ]


def swap(value, axis, parity, reach=1):
    return lax.ppermute(value, axis, partners(axis, parity, reach))


def slip_kernel(
    place, cover_in, slip_in, green, h_in, m_in, n_in, w_in,
    msg_a, msg_b, far_a, far_b, own, held, cover, slip, edge_f, edge_i, sems,
):
    def fetch(slot):
        return pltpu.make_async_copy(green.at[slot], held.at[slot], sems.at[slot])

    small = [
        pltpu.make_async_copy(slip_in, slip, sems.at[9]),
        pltpu.make_async_copy(cover_in, cover, sems.at[10]),
    ]
    edges = []
    for f, field in enumerate((h_in, m_in, n_in, w_in)):
        for t, start in enumerate((0, ROWS - 8)):
            target = edge_f.at[f, t] if f < 3 else edge_i.at[t]
            edges.append(
                pltpu.make_async_copy(field.at[start : start + 8], target, sems.at[11 + 2 * f + t])
            )
    for copy in small:
        copy.start()
    order = (0, 6, 3, 1, 7, 4, 2, 8, 5)
    for slot in order:
        fetch(slot).start()
    for copy in edges:
        copy.start()
    for copy in small:
        copy.wait()
    even = place[0] % 2 == 0
    even2 = (place[0] // 2) % 2 == 0

    rates = slip[...].astype(jnp.float32)
    rates = jnp.concatenate([rates] * 8, axis=1)
    rates = jnp.concatenate(
        [jnp.broadcast_to(rates[s : s + 1], (8, 256)) for s in range(STEPS)], axis=0
    )
    row = lax.broadcasted_iota(jnp.int32, (32, 256), 0)
    col = lax.broadcasted_iota(jnp.int32, (32, 256), 1)
    spread = jnp.where(col // 32 == row % 8, rates, 0.0).astype(jnp.bfloat16)

    def group(slot, g):
        right = jnp.concatenate(
            [held[slot, :, (g * 8 + p) * LANES : (g * 8 + p + 1) * LANES] for p in range(8)],
            axis=0,
        )
        value = jnp.dot(spread, right, preferred_element_type=jnp.float32)
        return value * cover[0, slot].astype(jnp.float32)

    for b in range(3):
        fetch(b).wait()
        fetch(6 + b).wait()
        fetch(3 + b).wait()
        for g in range(8):
            up = group(b, g)
            down = group(6 + b, g)
            mid = group(3 + b, g)
            first = jnp.where(even, down, up)
            second = jnp.where(even, up, down)
            for s in range(STEPS):
                part = slice(8 * s, 8 * s + 8)
                at = s * UX + g * 8
                msg_a[b * MAIN + at : b * MAIN + at + 8, :] = first[part]
                msg_b[b * MAIN + at : b * MAIN + at + 8, :] = second[part]
                own[b, at : at + 8, :] = mid[part]
            if g == 0:
                for s in range(STEPS):
                    own[b, MAIN + s : MAIN + s + 1, :] = down[8 * s : 8 * s + 1]
                up_edge, up_mid = up, mid
            if g == 7:
                for s in range(STEPS):
                    own[b, MAIN + 4 + s : MAIN + 5 + s, :] = up[8 * s + 7 : 8 * s + 8]
                    at = b * STEPS + s
                    to_down = mid[8 * s + 7 : 8 * s + 8]
                    to_up = up_mid[8 * s : 8 * s + 1]
                    msg_a[SLIVER + at : SLIVER + at + 1, :] = jnp.where(even, to_down, to_up)
                    msg_b[SLIVER + at : SLIVER + at + 1, :] = jnp.where(even, to_up, to_down)
                    to_down = down[8 * s + 7 : 8 * s + 8]
                    to_up = up_edge[8 * s : 8 * s + 1]
                    far_a[at : at + 1, :] = jnp.where(even2, to_down, to_up)
                    far_b[at : at + 1, :] = jnp.where(even2, to_up, to_down)
    blank = jnp.zeros((4, LANES), jnp.float32)
    for ref, start in ((msg_a, SLIVER), (msg_b, SLIVER), (far_a, 0), (far_b, 0)):
        ref[start + 12 : start + 16, :] = blank

    for copy in edges:
        copy.wait()
    for f in range(4):
        top, bottom = (edge_f[f, 0], edge_f[f, 1]) if f < 3 else (edge_i[0], edge_i[1])
        to_up = top[0:4].astype(jnp.float32)
        to_down = bottom[4:8].astype(jnp.float32)
        first = jnp.where(even, to_down, to_up)
        second = jnp.where(even, to_up, to_down)
        for k in range(4):
            at = EDGE + (f * 4 + k) * 4
            msg_a[at : at + 4, :] = first[:, k * LANES : (k + 1) * LANES]
            msg_b[at : at + 4, :] = second[:, k * LANES : (k + 1) * LANES]


def column_kernel(
    place, own, got_a, got_b, gotfar_a, gotfar_b, h_l, h_r, m_l, m_r, n_l, n_r, w_l, w_r,
    msg_a, msg_b, far_a, far_b, centre, ring, edges, lanes,
):
    i, j = place[0], place[1]
    even = i % 2 == 0
    even2 = (i // 2) % 2 == 0
    above_ok, below_ok = i > 0, i < SIDE - 1
    above2_ok, below2_ok = i > 1, i < SIDE - 2
    even_j = j % 2 == 0
    even2_j = (j // 2) % 2 == 0

    lane = lax.broadcasted_iota(jnp.int32, (EXT, LANES), 1)

    def from_above(rows):
        return jnp.where(even, got_b[rows, :], got_a[rows, :])

    def from_below(rows):
        return jnp.where(even, got_a[rows, :], got_b[rows, :])

    sums = []
    for b in range(3):
        rows = slice(b * MAIN, (b + 1) * MAIN)
        main = own[b, 0:MAIN, :]
        main = main + jnp.where(above_ok, from_above(rows), 0.0)
        main = main + jnp.where(below_ok, from_below(rows), 0.0)
        rows = slice(SLIVER + 4 * b, SLIVER + 4 * b + 4)
        far = slice(4 * b, 4 * b + 4)
        above = jnp.where(above_ok, from_above(rows), 0.0)
        above = above + jnp.where(
            above2_ok, jnp.where(even2, gotfar_b[far, :], gotfar_a[far, :]), 0.0
        )
        below = jnp.where(below_ok, from_below(rows), 0.0)
        below = below + jnp.where(
            below2_ok, jnp.where(even2, gotfar_a[far, :], gotfar_b[far, :]), 0.0
        )
        tail = own[b, MAIN:RING, :] + jnp.concatenate([below, above], axis=0)
        sums.append(jnp.concatenate([main, tail], axis=0))
    left_sum, mid_sum, right_sum = sums

    msg_a[0:RING, :] = jnp.where(even_j, right_sum, left_sum)
    msg_b[0:RING, :] = jnp.where(even_j, left_sum, right_sum)
    centre[...] = mid_sum

    for f in range(4):
        for k in range(4):
            rows = slice(EDGE + (f * 4 + k) * 4, EDGE + (f * 4 + k) * 4 + 4)
            edges[f, :, k * LANES : (k + 1) * LANES] = jnp.concatenate(
                [from_below(rows), from_above(rows)], axis=0
            )

    packed = jnp.zeros((EXT, LANES), jnp.float32)

    def place_lanes(packed, block, source, target, count):
        moved = pltpu.roll(block, (target - source) % LANES, 1) if target != source else block
        return jnp.where((lane >= target) & (lane < target + count), moved, packed)

    fields = ((h_l, h_r), (m_l, m_r), (n_l, n_r), (w_l, w_r))
    for f, (left, right) in enumerate(fields):
        lo = jnp.concatenate([left[...].astype(jnp.float32), edges[f, :, 0:LANES]], axis=0)
        hi = jnp.concatenate(
            [right[...].astype(jnp.float32), edges[f, :, COLS - LANES : COLS]], axis=0
        )
        packed = place_lanes(packed, hi, LANES - 4, 4 * f, 4)
        packed = place_lanes(packed, lo, 0, 16 + 4 * f, 4)
    packed = place_lanes(packed, mid_sum, LANES - 1, 12, 1)
    packed = place_lanes(packed, mid_sum, 0, 31, 1)
    packed = place_lanes(packed, right_sum, LANES - 1, 32, 1)
    packed = place_lanes(packed, left_sum, 0, 33, 1)
    packed = place_lanes(packed, left_sum, LANES - 1, 34, 1)
    packed = place_lanes(packed, right_sum, 0, 35, 1)
    lanes[0:EXT, :] = packed
    lanes[EXT:384, :] = jnp.zeros((384 - EXT, LANES), jnp.float32)

    zero8 = jnp.zeros((8, LANES), jnp.float32)
    far_a[...] = zero8
    far_b[...] = zero8
    ring[...] = zero8
    for k in range(3):
        turned = lanes[k * LANES : (k + 1) * LANES, :].T
        at = TURNED + 16 * k
        msg_a[at : at + 16, :] = jnp.where(even_j, turned[0:16], turned[16:32])
        msg_b[at : at + 16, :] = jnp.where(even_j, turned[16:32], turned[0:16])
        far_a[k : k + 1, :] = jnp.where(even2_j, turned[32:33], turned[33:34])
        far_b[k : k + 1, :] = jnp.where(even2_j, turned[33:34], turned[32:33])
        ring[k : k + 1, :] = turned[34:35]
        ring[4 + k : 5 + k, :] = turned[35:36]


def step_kernel(
    place, centre, got_a, got_b, gotfar_a, gotfar_b, ring, edges, h_in, m_in, n_in, w_in,
    h_out, m_out, n_out, state_a, state_b, wet, lift, turned,
):
    i, j = place[0], place[1]
    even_j = j % 2 == 0
    even2_j = (j // 2) % 2 == 0
    top, bottom = i == 0, i == SIDE - 1
    left_end, right_end = j == 0, j == SIDE - 1

    def from_left(rows):
        return jnp.where(even_j, got_b[rows, :], got_a[rows, :])

    def from_right(rows):
        return jnp.where(even_j, got_a[rows, :], got_b[rows, :])

    rows = slice(0, RING)
    total = centre[...] + jnp.where(left_end, 0.0, from_left(rows))
    total = 0.05 * (total + jnp.where(right_end, 0.0, from_right(rows)))
    coarse = lax.broadcasted_iota(jnp.int32, (LANES, COLS), 0)
    fine = lax.broadcasted_iota(jnp.int32, (LANES, COLS), 1)
    spread = jnp.where(fine // 4 == coarse, 1.0, 0.0).astype(jnp.bfloat16)
    part = total.astype(jnp.bfloat16)
    rest = total - part.astype(jnp.float32)
    part2 = rest.astype(jnp.bfloat16)
    part3 = (rest - part2.astype(jnp.float32)).astype(jnp.bfloat16)
    dot = functools.partial(jnp.dot, preferred_element_type=jnp.float32)
    lift[:, 0:COLS] = dot(part, spread) + dot(part2, spread) + dot(part3, spread)

    turned[40:LANES, :] = jnp.zeros((LANES - 40, LANES), jnp.float32)
    beside = []
    for k in range(3):
        at = TURNED + 16 * k
        left = from_left(slice(at, at + 16))
        right = from_right(slice(at, at + 16))
        for f in range(4):
            turned[8 * f : 8 * f + 4, :] = left[4 * f : 4 * f + 4]
            turned[8 * f + 4 : 8 * f + 8, :] = right[4 * f : 4 * f + 4]
        far_left = jnp.where(even2_j, gotfar_b[k : k + 1, :], gotfar_a[k : k + 1, :])
        far_right = jnp.where(even2_j, gotfar_a[k : k + 1, :], gotfar_b[k : k + 1, :])
        ring_left = ring[k : k + 1, :] + left[12:13] + jnp.where(j > 1, far_left, 0.0)
        ring_right = ring[4 + k : 5 + k, :] + right[15:16]
        ring_right = ring_right + jnp.where(j < SIDE - 2, far_right, 0.0)
        turned[32:36, :] = jnp.broadcast_to(0.05 * ring_left, (4, LANES))
        turned[36:40, :] = jnp.broadcast_to(0.05 * ring_right, (4, LANES))
        beside.append(turned[...].T)
    beside = jnp.concatenate([beside[0], beside[1], beside[2][0:8]], axis=0)

    def side_block(f):
        return pltpu.roll(beside, (LANES - 4 - 8 * f) % LANES, 1)

    for f, field in enumerate((h_in, m_in, n_in)):
        state_a[f, 0:ROWS, 0:COLS] = field[...]
        state_a[f, ROWS:EXT, 0:COLS] = edges[f]
        state_a[f, :, COLS:WIDE] = side_block(f)
    wet[0:ROWS, 0:COLS] = w_in[...].astype(jnp.float32)
    wet[ROWS:EXT, 0:COLS] = edges[3]
    wet[:, COLS:WIDE] = side_block(3)
    lift[:, COLS:WIDE] = side_block(4)

    sub = lax.broadcasted_iota(jnp.int32, (8, WIDE), 0)
    first_row, last_row, upper_half = sub == 0, sub == 7, sub < 4
    lane = lax.broadcasted_iota(jnp.int32, (8, LANES), 1)
    lane_left = (lane == LANES - 1) & left_end
    lane_right = (lane == 0) & right_end

    def load(ref, f, at):
        value = ref[f, pl.ds(at, 8), :]
        block = value[:, COLS:WIDE]
        block = jnp.where(lane_left, pltpu.roll(value[:, 0:LANES], LANES - 1, 1), block)
        block = jnp.where(lane_right, pltpu.roll(value[:, COLS - LANES : COLS], 1, 1), block)
        return jnp.concatenate([value[:, 0:COLS], block], axis=1)

    def fluxes(ref, at):
        height, east, north = load(ref, 0, at), load(ref, 1, at), load(ref, 2, at)
        inverse = 1.0 / height
        v = north * inverse
        pressure = 0.05 * height * height
        fm = 0.1 * east
        gn = 0.1 * north
        fmm = fm * (east * inverse) + pressure
        fmn = fm * v
        gnn = gn * v + pressure
        quarter = (0.25 * height, 0.25 * east, 0.25 * north)
        return quarter, (fm, fmm, fmn), (gn, fmn, gnn)

    def down_shift(quarter, flux):
        return [pltpu.roll(q + x, 1, 0) for q, x in zip(quarter, flux)]

    def up_shift(quarter, flux):
        return [pltpu.roll(q - x, 7, 0) for q, x in zip(quarter, flux)]

    def across(quarter, flux):
        return [
            pltpu.roll(q - x, WIDE - 1, 1) + pltpu.roll(q + x, 1, 1)
            for q, x in zip(quarter, flux)
        ]

    zeros = jnp.zeros((8, WIDE), jnp.float32)

    for s in range(STEPS):
        source, target = (state_a, state_b) if s % 2 == 0 else (state_b, state_a)
        final = s == STEPS - 1
        for f in range(3):
            source[f, EXT - 1 : EXT, :] = jnp.where(
                top, source[f, 0:1, :], source[f, EXT - 1 : EXT, :]
            )
            source[f, ROWS : ROWS + 1, :] = jnp.where(
                bottom, source[f, ROWS - 1 : ROWS, :], source[f, ROWS : ROWS + 1, :]
            )

        def visit(at, above, source=source):
            quarter, east_flux, north_flux = fluxes(source, at)
            below = down_shift(quarter, east_flux)
            ahead = up_shift(quarter, east_flux)
            partial = [
                w + jnp.where(first_row, a, b) + jnp.where(last_row, 0.0, u)
                for w, a, b, u in zip(across(quarter, north_flux), above, below, ahead)
            ]
            return partial, below, ahead

        def finish(at, upper, lower, partial, ahead, s=s, final=final, target=target):
            height, east, north = [
                p + jnp.where(last_row, u, 0.0) for p, u in zip(partial, ahead)
            ]
            raised = jnp.where(
                upper_half,
                jnp.broadcast_to(lift[pl.ds(upper, 1), :], (8, WIDE)),
                jnp.broadcast_to(lift[pl.ds(lower, 1), :], (8, WIDE)),
            )
            height = height + raised
            mask = wet[pl.ds(at, 8), :]
            east = east * mask
            north = north * mask
            if final:
                h_out[pl.ds(at, 8), :] = height[:, 0:COLS]
                m_out[pl.ds(at, 8), :] = east[:, 0:COLS]
                n_out[pl.ds(at, 8), :] = north[:, 0:COLS]
            else:
                target[0, pl.ds(at, 8), :] = height
                target[1, pl.ds(at, 8), :] = east
                target[2, pl.ds(at, 8), :] = north

        quarter, east_flux, _ = fluxes(source, ROWS)
        above = down_shift(quarter, east_flux)
        partial, above, _ = visit(0, above)

        def body(c, carry, visit=visit, finish=finish, s=s):
            partial, above = carry
            at = pl.multiple_of(c * 8, 8)
            new_partial, new_above, ahead = visit(at, above)
            before = pl.multiple_of(at - 8, 8)
            row = s * UX + 2 * (c - 1)
            finish(before, row, row + 1, partial, ahead)
            return new_partial, new_above

        partial, above = lax.fori_loop(1, EXT // 8, body, (partial, above), unroll=UNROLL)
        if not final:
            quarter, east_flux, _ = fluxes(source, 0)
            ahead = up_shift(quarter, east_flux)
            finish(ROWS, MAIN + s, MAIN + 4 + s, partial, ahead)


def whole(shape):
    return pl.BlockSpec(shape, lambda g: (0,) * len(shape))


def smem():
    return pl.BlockSpec(memory_space=pltpu.SMEM)


def f32(*shape):
    return jax.ShapeDtypeStruct(shape, jnp.float32)


def run(body, outs, in_specs, scratch, args, name):
    return pl.pallas_call(
        body,
        grid=(1,),
        in_specs=in_specs,
        out_specs=[whole(o.shape) for o in outs],
        out_shape=outs,
        scratch_shapes=scratch,
        compiler_params=pltpu.CompilerParams(vmem_limit_bytes=VMEM_LIMIT),
        name=name,
    )(*args)


def shards(slip_rate, green_kernel, intersection, wet_mask, column_height, east_flow, north_flow):
    place = jnp.stack([lax.axis_index("ox"), lax.axis_index("oy")]).astype(jnp.int32)
    fields = (column_height, east_flow, north_flow, wet_mask)

    far_away = pl.BlockSpec(memory_space=pltpu.HBM)
    msg_a, msg_b, far_a, far_b, own = run(
        slip_kernel,
        [f32(ROW_MSG, LANES)] * 2 + [f32(16, LANES)] * 2 + [f32(3, RING, LANES)],
        [smem()] + [far_away] * 7,
        [
            pltpu.VMEM((9, 32, UX * LANES), jnp.bfloat16),
            pltpu.SMEM((1, 9), jnp.int32),
            pltpu.VMEM((STEPS, 32), jnp.bfloat16),
            pltpu.VMEM((3, 2, 8, COLS), jnp.float32),
            pltpu.VMEM((2, 8, COLS), jnp.int32),
            pltpu.SemaphoreType.DMA((19,)),
        ],
        (place,)
        + tuple(
            pltpu.with_memory_space_constraint(x, pltpu.HBM)
            for x in (intersection, slip_rate, jnp.transpose(green_kernel, (1, 0, 2))) + fields
        ),
        "slip",
    )
    got_a = swap(msg_a, "ox", 0)
    got_b = swap(msg_b, "ox", 1)
    gotfar_a = swap(far_a, "ox", 0, 2)
    gotfar_b = swap(far_b, "ox", 1, 2)

    side = [pl.BlockSpec((ROWS, LANES), lambda g: (0, 0)), pl.BlockSpec((ROWS, LANES), lambda g: (0, COLS // LANES - 1))]
    msg_a, msg_b, far_a, far_b, centre, ring, edges = run(
        column_kernel,
        [f32(COL_MSG, LANES)] * 2 + [f32(8, LANES)] * 2 + [f32(RING, LANES), f32(8, LANES), f32(4, 8, COLS)],
        [smem(), whole((3, RING, LANES))] + [whole((ROW_MSG, LANES))] * 2 + [whole((16, LANES))] * 2 + side * 4,
        [pltpu.VMEM((384, LANES), jnp.float32)],
        (place, own, got_a, got_b, gotfar_a, gotfar_b) + tuple(x for x in fields for _ in range(2)),
        "column",
    )
    got_a = swap(msg_a, "oy", 0)
    got_b = swap(msg_b, "oy", 1)
    gotfar_a = swap(far_a, "oy", 0, 2)
    gotfar_b = swap(far_b, "oy", 1, 2)

    tile = whole((ROWS, COLS))
    return tuple(
        run(
            step_kernel,
            [f32(ROWS, COLS)] * 3,
            [smem(), whole((RING, LANES))] + [whole((COL_MSG, LANES))] * 2 + [whole((8, LANES))] * 3
            + [whole((4, 8, COLS))] + [tile] * 4,
            [
                pltpu.VMEM((3, EXT, WIDE), jnp.float32),
                pltpu.VMEM((3, EXT, WIDE), jnp.float32),
                pltpu.VMEM((EXT, WIDE), jnp.float32),
                pltpu.VMEM((EXT, WIDE), jnp.float32),
                pltpu.VMEM((LANES, LANES), jnp.float32),
            ],
            (place, centre, got_a, got_b, gotfar_a, gotfar_b, ring, edges) + fields[:3] + (wet_mask,),
            "step",
        )
    )


def solution(mesh):
    return jax.shard_map(
        shards,
        mesh=mesh,
        in_specs=(
            P(None, ("ox", "oy")),
            P(("ox", "oy"), None, None),
            P(("ox", "oy"), None),
            P("ox", "oy"),
            P("ox", "oy"),
            P("ox", "oy"),
            P("ox", "oy"),
        ),
        out_specs=(P("ox", "oy"), P("ox", "oy"), P("ox", "oy")),
        check_vma=False,
    )
```

```python
import functools

import jax
import jax.numpy as jnp
from jax import lax
from jax.experimental import pallas as pl
from jax.experimental.pallas import tpu as pltpu
from jax.sharding import PartitionSpec as P

STEPS = 4
SIDE = 16
ROWS = 256
COLS = 512
LANES = 128
UX = 64
MAIN = STEPS * UX
RING = MAIN + 8
SLIVER = 2 * MAIN
EDGE = SLIVER + 16
RIM = EDGE + 64
ROW_MSG = RIM + 8
TURNED = RING
COL_MSG = RING + 48
MID_MSG = COL_MSG + 8
TALL = 3 * LANES
UNROLL = 4
VMEM_LIMIT = 48 * 1024 * 1024


def partners(axis, parity, reach):
    return [
        (i, (i + reach if (i // reach) % 2 == parity else i - reach) % SIDE)
        for i in range(SIDE)
    ]


def swap(value, axis, parity, reach=1):
    return lax.ppermute(value, axis, partners(axis, parity, reach))


def slip_kernel(
    place, cover_in, slip_in, green, h_in, m_in, n_in, w_in,
    msg_a, msg_b, mid_a, mid_b, far_a, far_b, own, rim, held, cover, slip, edge_f, edge_i, lanes, sems,
):
    def fetch(slot):
        return pltpu.make_async_copy(green.at[slot], held.at[slot], sems.at[slot])

    small = [
        pltpu.make_async_copy(slip_in, slip, sems.at[9]),
        pltpu.make_async_copy(cover_in, cover, sems.at[10]),
    ]
    edges = []
    for f, field in enumerate((h_in, m_in, n_in, w_in)):
        for t, start in enumerate((0, ROWS - 8)):
            target = edge_f.at[f, t] if f < 3 else edge_i.at[t]
            edges.append(
                pltpu.make_async_copy(field.at[start : start + 8], target, sems.at[11 + 2 * f + t])
            )
    for copy in small:
        copy.start()
    order = (0, 6, 3, 1, 7, 4, 2, 8, 5)
    for slot in order:
        fetch(slot).start()
    for copy in edges:
        copy.start()
    for copy in small:
        copy.wait()
    even = place[0] % 2 == 0
    even2 = (place[0] // 2) % 2 == 0

    rates = slip[...].astype(jnp.float32)
    rates = jnp.concatenate([rates] * 8, axis=1)
    rates = jnp.concatenate(
        [jnp.broadcast_to(rates[s : s + 1], (8, 256)) for s in range(STEPS)], axis=0
    )
    row = lax.broadcasted_iota(jnp.int32, (32, 256), 0)
    col = lax.broadcasted_iota(jnp.int32, (32, 256), 1)
    spread = jnp.where(col // 32 == row % 8, rates, 0.0).astype(jnp.bfloat16)
    lane = lax.broadcasted_iota(jnp.int32, (32, LANES), 1)

    def group(slot, g):
        right = jnp.concatenate(
            [held[slot, :, (g * 8 + p) * LANES : (g * 8 + p + 1) * LANES] for p in range(8)],
            axis=0,
        )
        value = jnp.dot(spread, right, preferred_element_type=jnp.float32)
        return value * cover[0, slot].astype(jnp.float32)

    def rims(down, up, mid):
        value = jnp.where(lane == 1, pltpu.roll(up, 1, 1), down)
        value = jnp.where(lane == LANES - 2, pltpu.roll(up, LANES - 1, 1), value)
        value = jnp.where(lane == 2, pltpu.roll(mid, 2, 1), value)
        return jnp.where(lane == LANES - 3, pltpu.roll(mid, LANES - 2, 1), value)

    for b in range(3):
        fetch(b).wait()
        fetch(6 + b).wait()
        fetch(3 + b).wait()
        to_a, to_b, base = ((msg_a, msg_b, 0), (mid_a, mid_b, 0), (msg_a, msg_b, MAIN))[b]
        for g in range(8):
            up = group(b, g)
            down = group(6 + b, g)
            mid = group(3 + b, g)
            first = jnp.where(even, down, up)
            second = jnp.where(even, up, down)
            if b == 1:
                rim_lanes = rims(down, up, mid)
            for s in range(STEPS):
                part = slice(8 * s, 8 * s + 8)
                at = s * UX + g * 8
                to_a[base + at : base + at + 8, :] = first[part]
                to_b[base + at : base + at + 8, :] = second[part]
                own[b, at : at + 8, :] = mid[part]
                if b == 1:
                    lanes[at : at + 8, :] = rim_lanes[part]
            if g == 0:
                for s in range(STEPS):
                    own[b, MAIN + s : MAIN + s + 1, :] = down[8 * s : 8 * s + 1]
                up_edge, up_mid = up, mid
            if g == 7:
                for s in range(STEPS):
                    own[b, MAIN + 4 + s : MAIN + 5 + s, :] = up[8 * s + 7 : 8 * s + 8]
                    at = b * STEPS + s
                    to_down = mid[8 * s + 7 : 8 * s + 8]
                    to_up = up_mid[8 * s : 8 * s + 1]
                    msg_a[SLIVER + at : SLIVER + at + 1, :] = jnp.where(even, to_down, to_up)
                    msg_b[SLIVER + at : SLIVER + at + 1, :] = jnp.where(even, to_up, to_down)
                    to_down = down[8 * s + 7 : 8 * s + 8]
                    to_up = up_edge[8 * s : 8 * s + 1]
                    far_a[at : at + 1, :] = jnp.where(even2, to_down, to_up)
                    far_b[at : at + 1, :] = jnp.where(even2, to_up, to_down)
    blank = jnp.zeros((4, LANES), jnp.float32)
    for ref, start in ((msg_a, SLIVER + 12), (msg_b, SLIVER + 12), (far_a, 12), (far_b, 12)):
        ref[start : start + 4, :] = blank
    for ref, start in ((msg_a, RIM + 4), (msg_b, RIM + 4), (rim, 4)):
        ref[start : start + 4, :] = blank
    for ref in (mid_a, mid_b):
        ref[MAIN:MID_MSG, :] = jnp.zeros((MID_MSG - MAIN, LANES), jnp.float32)
    for k in range(2):
        turned = lanes[k * LANES : (k + 1) * LANES, :].T
        to_down = jnp.concatenate([turned[0:1], turned[127:128]], axis=0)
        to_up = jnp.concatenate([turned[1:2], turned[126:127]], axis=0)
        at = RIM + 2 * k
        msg_a[at : at + 2, :] = jnp.where(even, to_down, to_up)
        msg_b[at : at + 2, :] = jnp.where(even, to_up, to_down)
        rim[2 * k : 2 * k + 1, :] = turned[2:3]
        rim[2 * k + 1 : 2 * k + 2, :] = turned[125:126]

    for copy in edges:
        copy.wait()
    for f in range(4):
        top, bottom = (edge_f[f, 0], edge_f[f, 1]) if f < 3 else (edge_i[0], edge_i[1])
        to_up = top[0:4].astype(jnp.float32)
        to_down = bottom[4:8].astype(jnp.float32)
        first = jnp.where(even, to_down, to_up)
        second = jnp.where(even, to_up, to_down)
        for k in range(4):
            at = EDGE + (f * 4 + k) * 4
            msg_a[at : at + 4, :] = first[:, k * LANES : (k + 1) * LANES]
            msg_b[at : at + 4, :] = second[:, k * LANES : (k + 1) * LANES]


def column_kernel(
    place, _, own, rim, got_a, got_b, gotfar_a, gotfar_b, h_l, h_r, m_l, m_r, n_l, n_r, w_l, w_r,
    msg_a, msg_b, far_a, far_b, tail1, ring, turned_own, edges, lanes,
):
    i, j = place[0], place[1]
    even = i % 2 == 0
    even2 = (i // 2) % 2 == 0
    above_ok, below_ok = i > 0, i < SIDE - 1
    above2_ok, below2_ok = i > 1, i < SIDE - 2
    even_j = j % 2 == 0
    even2_j = (j // 2) % 2 == 0

    def from_above(rows):
        return jnp.where(even, got_b[rows, :], got_a[rows, :])

    def from_below(rows):
        return jnp.where(even, got_a[rows, :], got_b[rows, :])

    tails = []
    for b in range(3):
        rows = slice(SLIVER + 4 * b, SLIVER + 4 * b + 4)
        far = slice(4 * b, 4 * b + 4)
        above = jnp.where(above_ok, from_above(rows), 0.0)
        above = above + jnp.where(
            above2_ok, jnp.where(even2, gotfar_b[far, :], gotfar_a[far, :]), 0.0
        )
        below = jnp.where(below_ok, from_below(rows), 0.0)
        below = below + jnp.where(
            below2_ok, jnp.where(even2, gotfar_a[far, :], gotfar_b[far, :]), 0.0
        )
        tails.append(own[b, MAIN:RING, :] + jnp.concatenate([below, above], axis=0))
    tail1[...] = tails[1]

    sums = []
    for b, base in ((0, 0), (2, MAIN)):
        rows = slice(base, base + MAIN)
        main = own[b, 0:MAIN, :]
        main = main + jnp.where(above_ok, from_above(rows), 0.0)
        main = main + jnp.where(below_ok, from_below(rows), 0.0)
        sums.append(main)
    left_sum, right_sum = sums
    msg_a[0:MAIN, :] = jnp.where(even_j, right_sum, left_sum)
    msg_b[0:MAIN, :] = jnp.where(even_j, left_sum, right_sum)
    msg_a[MAIN:RING, :] = jnp.where(even_j, tails[2], tails[0])
    msg_b[MAIN:RING, :] = jnp.where(even_j, tails[0], tails[2])

    for f in range(4):
        for k in range(4):
            rows = slice(EDGE + (f * 4 + k) * 4, EDGE + (f * 4 + k) * 4 + 4)
            edges[f, :, k * LANES : (k + 1) * LANES] = jnp.concatenate(
                [from_below(rows), from_above(rows)], axis=0
            )

    def tuck(packed, lane, block, source, target, count):
        moved = pltpu.roll(block, (target - source) % LANES, 1) if target != source else block
        return jnp.where((lane >= target) & (lane < target + count), moved, packed)

    fields = ((h_l, h_r), (m_l, m_r), (n_l, n_r), (w_l, w_r))
    lane = lax.broadcasted_iota(jnp.int32, (ROWS, LANES), 1)
    packed = jnp.zeros((ROWS, LANES), jnp.float32)
    lane8 = lax.broadcasted_iota(jnp.int32, (8, LANES), 1)
    packed8 = jnp.zeros((8, LANES), jnp.float32)
    for f, (left, right) in enumerate(fields):
        packed = tuck(packed, lane, right[...].astype(jnp.float32), LANES - 8, 8 * f, 8)
        packed = tuck(packed, lane, left[...].astype(jnp.float32), 0, 32 + 8 * f, 8)
        packed8 = tuck(packed8, lane8, edges[f, :, COLS - LANES : COLS], LANES - 8, 8 * f, 8)
        packed8 = tuck(packed8, lane8, edges[f, :, 0:LANES], 0, 32 + 8 * f, 8)
    spots = ((2, LANES - 1, 64), (0, 0, 65), (0, LANES - 1, 66), (2, 0, 67))
    for b, source, target in spots:
        packed = tuck(packed, lane, sums[b // 2], source, target, 1)
        packed8 = tuck(packed8, lane8, tails[b], source, target, 1)
    packed8 = tuck(packed8, lane8, tails[1], 0, 68, 1)
    packed8 = tuck(packed8, lane8, tails[1], LANES - 1, 69, 1)
    lanes[0:ROWS, :] = packed
    lanes[ROWS : ROWS + 4, :] = packed8[0:4]
    lanes[ROWS + 4 : TALL - 4, :] = jnp.zeros((TALL - ROWS - 8, LANES), jnp.float32)
    lanes[TALL - 4 : TALL, :] = packed8[4:8]

    zero8 = jnp.zeros((8, LANES), jnp.float32)
    far_a[...] = zero8
    far_b[...] = zero8
    ring[...] = zero8
    for k in range(3):
        turned = lanes[k * LANES : (k + 1) * LANES, :].T
        turned_own[k] = turned[0:64]
        if k < 2:
            rims = []
            for side in range(2):
                row = slice(RIM + 2 * k + side, RIM + 2 * k + side + 1)
                value = rim[2 * k + side : 2 * k + side + 1, :]
                value = value + jnp.where(above_ok, from_above(row), 0.0)
                rims.append(value + jnp.where(below_ok, from_below(row), 0.0))
        else:
            rims = [turned[68:69], turned[69:70]]
        to_right = [turned[8 * f + 4 : 8 * f + 8] for f in range(3)] + [rims[1], turned[29:32]]
        to_left = [turned[32 + 8 * f : 36 + 8 * f] for f in range(3)] + [turned[56:59], rims[0]]
        to_right = jnp.concatenate(to_right, axis=0)
        to_left = jnp.concatenate(to_left, axis=0)
        at = TURNED + 16 * k
        msg_a[at : at + 16, :] = jnp.where(even_j, to_right, to_left)
        msg_b[at : at + 16, :] = jnp.where(even_j, to_left, to_right)
        far_a[k : k + 1, :] = jnp.where(even2_j, turned[64:65], turned[65:66])
        far_b[k : k + 1, :] = jnp.where(even2_j, turned[65:66], turned[64:65])
        ring[k : k + 1, :] = turned[66:67]
        ring[4 + k : 5 + k, :] = turned[67:68]


def spread_matrix():
    coarse = lax.broadcasted_iota(jnp.int32, (LANES, COLS), 0)
    fine = lax.broadcasted_iota(jnp.int32, (LANES, COLS), 1)
    return jnp.where(fine // 4 == coarse, 1.0, 0.0).astype(jnp.bfloat16)


def widen(value, spread):
    part = value.astype(jnp.bfloat16)
    rest = value - part.astype(jnp.float32)
    part2 = rest.astype(jnp.bfloat16)
    part3 = (rest - part2.astype(jnp.float32)).astype(jnp.bfloat16)
    dot = functools.partial(jnp.dot, preferred_element_type=jnp.float32)
    return dot(part, spread) + dot(part2, spread) + dot(part3, spread)


def fluxes(height, east, north):
    inverse = 1.0 / height
    v = north * inverse
    pressure = 0.05 * height * height
    fm = 0.1 * east
    gn = 0.1 * north
    fmm = fm * (east * inverse) + pressure
    fmn = fm * v
    gnn = gn * v + pressure
    quarter = (0.25 * height, 0.25 * east, 0.25 * north)
    return quarter, (fm, fmm, fmn), (gn, fmn, gnn)


def interior_step(load, store):
    sub = lax.broadcasted_iota(jnp.int32, (8, COLS), 0)
    first_row, last_row = sub == 0, sub == 7
    zeros = jnp.zeros((8, COLS), jnp.float32)

    def finish(at, partial, ahead):
        store(at, [p + jnp.where(last_row, u, 0.0) for p, u in zip(partial, ahead)])

    def body(c, carry):
        partial, above = carry
        at = pl.multiple_of(c * 8, 8)
        quarter, east_flux, north_flux = fluxes(*load(at))
        below = [pltpu.roll(q + x, 1, 0) for q, x in zip(quarter, east_flux)]
        ahead = [pltpu.roll(q - x, 7, 0) for q, x in zip(quarter, east_flux)]
        new_partial = [
            pltpu.roll(q - g, COLS - 1, 1)
            + pltpu.roll(q + g, 1, 1)
            + jnp.where(first_row, a, b)
            + jnp.where(last_row, 0.0, u)
            for q, g, a, b, u in zip(quarter, north_flux, above, below, ahead)
        ]
        finish(pl.multiple_of(jnp.maximum(c - 1, 0) * 8, 8), partial, ahead)
        return new_partial, below

    partial, _ = lax.fori_loop(0, ROWS // 8, body, ([zeros] * 3, [zeros] * 3), unroll=UNROLL)
    finish(ROWS - 8, partial, [zeros] * 3)


def first_kernel(h_in, m_in, n_in, moved):
    def load(at):
        return [ref[pl.ds(at, 8), :] for ref in (h_in, m_in, n_in)]

    def store(at, values):
        for f in range(3):
            moved[f, pl.ds(at, 8), :] = values[f]

    interior_step(load, store)


def main_kernel(
    place, own, mid_a, mid_b, got_a, got_b, moved, w_in,
    h_out, m_out, n_out, total, state, lift,
):
    i, j = place[0], place[1]
    even = i % 2 == 0
    even_j = j % 2 == 0
    rows = slice(0, MAIN)
    value = own[1, rows, :]
    value = value + jnp.where(i > 0, jnp.where(even, mid_b[rows, :], mid_a[rows, :]), 0.0)
    value = value + jnp.where(i < SIDE - 1, jnp.where(even, mid_a[rows, :], mid_b[rows, :]), 0.0)
    value = value + jnp.where(j > 0, jnp.where(even_j, got_b[rows, :], got_a[rows, :]), 0.0)
    value = value + jnp.where(
        j < SIDE - 1, jnp.where(even_j, got_a[rows, :], got_b[rows, :]), 0.0
    )
    total[...] = 0.05 * value
    lift[...] = widen(total[...], spread_matrix())
    upper_half = lax.broadcasted_iota(jnp.int32, (8, COLS), 0) < 4

    def source_and_mask(s, at, values):
        row = s * UX + at // 4
        raised = jnp.where(
            upper_half,
            jnp.broadcast_to(lift[pl.ds(row, 1), :], (8, COLS)),
            jnp.broadcast_to(lift[pl.ds(row + 1, 1), :], (8, COLS)),
        )
        mask = w_in[pl.ds(at, 8), :].astype(jnp.float32)
        return [values[0] + raised, values[1] * mask, values[2] * mask]

    for s in range(1, STEPS):

        def load(at, s=s):
            if s == 1:
                return source_and_mask(0, at, [moved[f, pl.ds(at, 8), :] for f in range(3)])
            return [state[s % 2, f, pl.ds(at, 8), :] for f in range(3)]

        def store(at, values, s=s):
            values = source_and_mask(s, at, values)
            for f in range(3):
                if s == STEPS - 1:
                    (h_out, m_out, n_out)[f][pl.ds(at, 8), :] = values[f]
                else:
                    state[(s + 1) % 2, f, pl.ds(at, 8), :] = values[f]

        interior_step(load, store)


def strip_kernel(
    place, total, tail1, got_a, got_b, gotfar_a, gotfar_b, ring, turned_own, edges,
    h_t, h_b, m_t, m_b, n_t, n_b, w_t, w_b, h_in, m_in, n_in,
    h_out, m_out, n_out, block,
):
    i, j = place[0], place[1]
    even_j = j % 2 == 0
    even2_j = (j // 2) % 2 == 0
    spread = spread_matrix()

    def from_left(rows):
        return jnp.where(even_j, got_b[rows, :], got_a[rows, :])

    def from_right(rows):
        return jnp.where(even_j, got_a[rows, :], got_b[rows, :])

    tail = tail1[...] + jnp.where(j > 0, from_left(slice(MAIN, RING)), 0.0)
    tail = 0.05 * (tail + jnp.where(j < SIDE - 1, from_right(slice(MAIN, RING)), 0.0))

    def six(values):
        return jnp.concatenate([jnp.broadcast_to(v, (4, v.shape[1])) for v in values], axis=0)

    coarse = []
    for s in range(STEPS):
        at = s * UX
        coarse += [
            tail[4 + s : 5 + s], total[at : at + 2, :], total[at + UX - 2 : at + UX, :], tail[s : s + 1],
        ]
    fine = widen(jnp.concatenate(coarse, axis=0), spread)
    row_lift = [
        six([fine[6 * s + r : 6 * s + r + 1] for r in range(6)]) for s in range(STEPS)
    ]
    row_state = []
    for f, (top, bottom) in enumerate(((h_t, h_b), (m_t, m_b), (n_t, n_b), (w_t, w_b))):
        row_state.append(
            jnp.concatenate(
                [
                    edges[f, 4:8, :],
                    top[...].astype(jnp.float32),
                    bottom[...].astype(jnp.float32),
                    edges[f, 0:4, :],
                ],
                axis=0,
            )
        )

    parts = [[], [], [], []]
    ups = []
    for k in range(3):
        at = TURNED + 16 * k
        left, right = from_left(slice(at, at + 16)), from_right(slice(at, at + 16))
        for f in range(4):
            parts[f].append(
                jnp.concatenate(
                    [
                        left[4 * f : 4 * f + 4],
                        turned_own[k, 32 + 8 * f : 40 + 8 * f, :],
                        turned_own[k, 8 * f : 8 * f + 8, :],
                        right[4 * f : 4 * f + 4],
                    ],
                    axis=0,
                )
            )
        far_left = jnp.where(even2_j, gotfar_b[k : k + 1, :], gotfar_a[k : k + 1, :])
        far_right = jnp.where(even2_j, gotfar_a[k : k + 1, :], gotfar_b[k : k + 1, :])
        ring_left = ring[k : k + 1, :] + left[12:13] + jnp.where(j > 1, far_left, 0.0)
        ring_right = ring[4 + k : 5 + k, :] + right[15:16]
        ring_right = ring_right + jnp.where(j < SIDE - 2, far_right, 0.0)
        if k < 2:
            turned = total[k * LANES : (k + 1) * LANES, :].T
        else:
            block[...] = jnp.zeros((LANES, LANES), jnp.float32)
            block[0:4, :] = tail[0:4]
            block[LANES - 4 : LANES, :] = tail[4:8]
            turned = block[...].T
        ups.append(
            jnp.concatenate(
                [0.05 * ring_left, turned[0:2], turned[126:128], 0.05 * ring_right, turned[0:2]],
                axis=0,
            )
        )
    col_state = [jnp.concatenate(p, axis=1) for p in parts]
    lane = lax.broadcasted_iota(jnp.int32, (8, LANES), 1)
    col_lift = []
    for s in range(STEPS):
        if s % 2 == 0:
            wide = widen(ups[s // 2], spread)
        own_rows = wide[:, 256 * (s % 2) : 256 * (s % 2) + 256]
        beside = jnp.where(
            lane < 4,
            jnp.broadcast_to(ups[2][:, s : s + 1], (8, LANES)),
            jnp.broadcast_to(ups[2][:, LANES - 4 + s : LANES - 3 + s], (8, LANES)),
        )
        both = jnp.concatenate([own_rows, beside], axis=1)
        col_lift.append(six([both[r : r + 1] for r in range(6)]))

    def advance(state, lift, wet, x_axis, ends):
        n_sub, n_lane = state[0].shape
        sub = lax.broadcasted_iota(jnp.int32, (n_sub, n_lane), 0)
        lanes = lax.broadcasted_iota(jnp.int32, (n_sub, n_lane), 1)
        fixed = []
        for value in state:
            value = jnp.where((sub == 3) & ends[0], pltpu.roll(value, n_sub - 1, 0), value)
            value = jnp.where((sub == 20) & ends[1], pltpu.roll(value, 1, 0), value)
            if len(ends) == 4:
                value = jnp.where((lanes == n_lane - 1) & ends[2], pltpu.roll(value, n_lane - 1, 1), value)
                value = jnp.where((lanes == ROWS) & ends[3], pltpu.roll(value, 1, 1), value)
            fixed.append(value)
        quarter, east_flux, north_flux = fluxes(*fixed)
        along_sub, along_lane = (east_flux, north_flux) if x_axis == 0 else (north_flux, east_flux)
        out = [
            pltpu.roll(q - a, n_sub - 1, 0)
            + pltpu.roll(q + a, 1, 0)
            + pltpu.roll(q - l, n_lane - 1, 1)
            + pltpu.roll(q + l, 1, 1)
            for q, a, l in zip(quarter, along_sub, along_lane)
        ]
        return [out[0] + lift, out[1] * wet, out[2] * wet]

    row_ends = (i == 0, i == SIDE - 1)
    col_ends = (j == 0, j == SIDE - 1) + row_ends
    rows, cols = row_state[:3], col_state[:3]
    for s in range(STEPS):
        rows = advance(rows, row_lift[s], row_state[3], 0, row_ends)
        cols = advance(cols, col_lift[s], col_state[3], 1, col_ends)

    lane = lax.broadcasted_iota(jnp.int32, (ROWS, LANES), 1)
    for f, (source, target) in enumerate(((h_in, h_out), (m_in, m_out), (n_in, n_out))):
        block[8 * f : 8 * f + 4, :] = cols[f][16:20, 0:LANES]
        block[8 * f + 4 : 8 * f + 8, :] = cols[f][4:8, 0:LANES]
    upper = block[...].T
    for f in range(3):
        block[8 * f : 8 * f + 4, :] = cols[f][16:20, LANES : 2 * LANES]
        block[8 * f + 4 : 8 * f + 8, :] = cols[f][4:8, LANES : 2 * LANES]
    rim = jnp.concatenate([upper, block[...].T], axis=0)
    for f, (source, target) in enumerate(((h_in, h_out), (m_in, m_out), (n_in, n_out))):
        value = jnp.concatenate(
            [rows[f][4:8], source[4 : ROWS - 4, :], rows[f][16:20]], axis=0
        )
        side = pltpu.roll(rim, (LANES - 4 - 8 * f) % LANES, 1)
        target[:, 0:LANES] = jnp.where(lane < 4, side, value[:, 0:LANES])
        target[:, LANES : COLS - LANES] = value[:, LANES : COLS - LANES]
        target[:, COLS - LANES : COLS] = jnp.where(
            lane >= LANES - 4, side, value[:, COLS - LANES : COLS]
        )


def whole(shape):
    return pl.BlockSpec(shape, lambda g: (0,) * len(shape))


def smem():
    return pl.BlockSpec(memory_space=pltpu.SMEM)


def f32(*shape):
    return jax.ShapeDtypeStruct(shape, jnp.float32)


def run(body, outs, in_specs, scratch, args, name, cost=None):
    if cost is not None:
        cost = pl.CostEstimate(flops=cost, bytes_accessed=0, transcendentals=0)
    return pl.pallas_call(
        body,
        grid=(1,),
        in_specs=in_specs,
        out_specs=[whole(o.shape) for o in outs],
        out_shape=outs,
        scratch_shapes=scratch,
        compiler_params=pltpu.CompilerParams(vmem_limit_bytes=VMEM_LIMIT),
        cost_estimate=cost,
        name=name,
    )(*args)


def shards(slip_rate, green_kernel, intersection, wet_mask, column_height, east_flow, north_flow):
    place = jnp.stack([lax.axis_index("ox"), lax.axis_index("oy")]).astype(jnp.int32)
    fields = (column_height, east_flow, north_flow, wet_mask)
    twice = tuple(x for x in fields for _ in range(2))

    far_away = pl.BlockSpec(memory_space=pltpu.HBM)
    msg_a, msg_b, mid_a, mid_b, far_a, far_b, own, rim = run(
        slip_kernel,
        [f32(ROW_MSG, LANES)] * 2 + [f32(MID_MSG, LANES)] * 2 + [f32(16, LANES)] * 2
        + [f32(3, RING, LANES), f32(8, LANES)],
        [smem()] + [far_away] * 7,
        [
            pltpu.VMEM((9, 32, UX * LANES), jnp.bfloat16),
            pltpu.SMEM((1, 9), jnp.int32),
            pltpu.VMEM((STEPS, 32), jnp.bfloat16),
            pltpu.VMEM((3, 2, 8, COLS), jnp.float32),
            pltpu.VMEM((2, 8, COLS), jnp.int32),
            pltpu.VMEM((MAIN, LANES), jnp.float32),
            pltpu.SemaphoreType.DMA((19,)),
        ],
        (place,)
        + tuple(
            pltpu.with_memory_space_constraint(x, pltpu.HBM)
            for x in (intersection, slip_rate, jnp.transpose(green_kernel, (1, 0, 2))) + fields
        ),
        "slip",
    )
    got_a = swap(msg_a, "ox", 0)
    got_b = swap(msg_b, "ox", 1)
    gotfar_a = swap(far_a, "ox", 0, 2)
    gotfar_b = swap(far_b, "ox", 1, 2)
    mid_a = swap(mid_a, "ox", 0)
    mid_b = swap(mid_b, "ox", 1)

    side = [
        pl.BlockSpec((ROWS, LANES), lambda g: (0, 0)),
        pl.BlockSpec((ROWS, LANES), lambda g: (0, COLS // LANES - 1)),
    ]
    tile = whole((ROWS, COLS))
    (moved,) = run(
        first_kernel, [f32(3, ROWS, COLS)], [tile] * 3, [], fields[:3], "first", None
    )
    msg_a, msg_b, far_a, far_b, tail1, ring, turned_own, edges = run(
        column_kernel,
        [f32(COL_MSG, LANES)] * 2 + [f32(8, LANES)] * 4 + [f32(3, 64, LANES), f32(4, 8, COLS)],
        [smem(), pl.BlockSpec(memory_space=pl.ANY), whole((3, RING, LANES)), whole((8, LANES))]
        + [whole((ROW_MSG, LANES))] * 2
        + [whole((16, LANES))] * 2 + side * 4,
        [pltpu.VMEM((TALL, LANES), jnp.float32)],
        (place, moved, own, rim, got_a, got_b, gotfar_a, gotfar_b) + twice,
        "column",
        10000000000,
    )
    got_a = swap(msg_a, "oy", 0)
    got_b = swap(msg_b, "oy", 1)
    gotfar_a = swap(far_a, "oy", 0, 2)
    gotfar_b = swap(far_b, "oy", 1, 2)

    height, east, north, total = run(
        main_kernel,
        [f32(ROWS, COLS)] * 3 + [f32(MAIN, LANES)],
        [smem(), whole((3, RING, LANES))] + [whole((MID_MSG, LANES))] * 2
        + [whole((COL_MSG, LANES))] * 2 + [whole((3, ROWS, COLS)), tile],
        [
            pltpu.VMEM((2, 3, ROWS, COLS), jnp.float32),
            pltpu.VMEM((MAIN, COLS), jnp.float32),
        ],
        (place, own, mid_a, mid_b, got_a, got_b, moved, wet_mask),
        "main",
        10000000000,
    )
    ends = [
        pl.BlockSpec((8, COLS), lambda g: (0, 0)),
        pl.BlockSpec((8, COLS), lambda g: (ROWS // 8 - 1, 0)),
    ]
    return tuple(
        run(
            strip_kernel,
            [f32(ROWS, COLS)] * 3,
            [smem(), whole((MAIN, LANES)), whole((8, LANES))] + [whole((COL_MSG, LANES))] * 2
            + [whole((8, LANES))] * 3 + [whole((3, 64, LANES)), whole((4, 8, COLS))] + ends * 4
            + [tile] * 3,
            [pltpu.VMEM((LANES, LANES), jnp.float32)],
            (place, total, tail1, got_a, got_b, gotfar_a, gotfar_b, ring, turned_own, edges)
            + twice + (height, east, north),
            "strip",
        )
    )


def solution(mesh):
    return jax.shard_map(
        shards,
        mesh=mesh,
        in_specs=(
            P(None, ("ox", "oy")),
            P(("ox", "oy"), None, None),
            P(("ox", "oy"), None),
            P("ox", "oy"),
            P("ox", "oy"),
            P("ox", "oy"),
            P("ox", "oy"),
        ),
        out_specs=(P("ox", "oy"), P("ox", "oy"), P("ox", "oy")),
        check_vma=False,
    )
```

```python
import functools

import jax
import jax.numpy as jnp
from jax import lax
from jax.experimental import pallas as pl
from jax.experimental.pallas import tpu as pltpu
from jax.sharding import PartitionSpec as P

STEPS = 4
SIDE = 16
ROWS = 256
COLS = 512
LANES = 128
UX = 64
MAIN = STEPS * UX
RING = MAIN + 8
SLIVER = 2 * MAIN
EDGE = SLIVER + 16
RIM = EDGE + 64
ROW_MSG = RIM + 8
TURNED = RING
COL_MSG = RING + 48
MID_MSG = COL_MSG + 8
TALL = 3 * LANES
UNROLL = 8
VMEM_LIMIT = 24 * 1024 * 1024


def partners(axis, parity, reach):
    return [
        (i, (i + reach if (i // reach) % 2 == parity else i - reach) % SIDE)
        for i in range(SIDE)
    ]


def swap(value, axis, parity, reach=1):
    return lax.ppermute(value, axis, partners(axis, parity, reach))


def slip_kernel(
    place, cover_in, slip_in, green, h_in, m_in, n_in, w_in,
    msg_a, msg_b, mid_a, mid_b, far_a, far_b, own, rim, held, cover, slip, edge_f, edge_i, lanes, sems,
):
    def fetch(slot):
        return pltpu.make_async_copy(green.at[slot], held.at[slot], sems.at[slot])

    small = [
        pltpu.make_async_copy(slip_in, slip, sems.at[9]),
        pltpu.make_async_copy(cover_in, cover, sems.at[10]),
    ]
    edges = []
    for f, field in enumerate((h_in, m_in, n_in, w_in)):
        for t, start in enumerate((0, ROWS - 8)):
            target = edge_f.at[f, t] if f < 3 else edge_i.at[t]
            edges.append(
                pltpu.make_async_copy(field.at[start : start + 8], target, sems.at[11 + 2 * f + t])
            )
    for copy in small:
        copy.start()
    order = (0, 6, 3, 1, 7, 4, 2, 8, 5)
    for slot in order:
        fetch(slot).start()
    for copy in edges:
        copy.start()
    for copy in small:
        copy.wait()
    even = place[0] % 2 == 0
    even2 = (place[0] // 2) % 2 == 0

    rates = slip[...].astype(jnp.float32)
    rates = jnp.concatenate([rates] * 8, axis=1)
    rates = jnp.concatenate(
        [jnp.broadcast_to(rates[s : s + 1], (8, 256)) for s in range(STEPS)], axis=0
    )
    row = lax.broadcasted_iota(jnp.int32, (32, 256), 0)
    col = lax.broadcasted_iota(jnp.int32, (32, 256), 1)
    spread = jnp.where(col // 32 == row % 8, rates, 0.0).astype(jnp.bfloat16)
    lane = lax.broadcasted_iota(jnp.int32, (32, LANES), 1)

    def group(slot, g):
        right = jnp.concatenate(
            [held[slot, :, (g * 8 + p) * LANES : (g * 8 + p + 1) * LANES] for p in range(8)],
            axis=0,
        )
        value = jnp.dot(spread, right, preferred_element_type=jnp.float32)
        return value * cover[0, slot].astype(jnp.float32)

    def rims(down, up, mid):
        value = jnp.where(lane == 1, pltpu.roll(up, 1, 1), down)
        value = jnp.where(lane == LANES - 2, pltpu.roll(up, LANES - 1, 1), value)
        value = jnp.where(lane == 2, pltpu.roll(mid, 2, 1), value)
        return jnp.where(lane == LANES - 3, pltpu.roll(mid, LANES - 2, 1), value)

    for b in range(3):
        fetch(b).wait()
        fetch(6 + b).wait()
        fetch(3 + b).wait()
        to_a, to_b, base = ((msg_a, msg_b, 0), (mid_a, mid_b, 0), (msg_a, msg_b, MAIN))[b]
        for g in range(8):
            up = group(b, g)
            down = group(6 + b, g)
            mid = group(3 + b, g)
            first = jnp.where(even, down, up)
            second = jnp.where(even, up, down)
            if b == 1:
                rim_lanes = rims(down, up, mid)
            for s in range(STEPS):
                part = slice(8 * s, 8 * s + 8)
                at = s * UX + g * 8
                to_a[base + at : base + at + 8, :] = first[part]
                to_b[base + at : base + at + 8, :] = second[part]
                own[b, at : at + 8, :] = mid[part]
                if b == 1:
                    lanes[at : at + 8, :] = rim_lanes[part]
            if g == 0:
                for s in range(STEPS):
                    own[b, MAIN + s : MAIN + s + 1, :] = down[8 * s : 8 * s + 1]
                up_edge, up_mid = up, mid
            if g == 7:
                for s in range(STEPS):
                    own[b, MAIN + 4 + s : MAIN + 5 + s, :] = up[8 * s + 7 : 8 * s + 8]
                    at = b * STEPS + s
                    to_down = mid[8 * s + 7 : 8 * s + 8]
                    to_up = up_mid[8 * s : 8 * s + 1]
                    msg_a[SLIVER + at : SLIVER + at + 1, :] = jnp.where(even, to_down, to_up)
                    msg_b[SLIVER + at : SLIVER + at + 1, :] = jnp.where(even, to_up, to_down)
                    to_down = down[8 * s + 7 : 8 * s + 8]
                    to_up = up_edge[8 * s : 8 * s + 1]
                    far_a[at : at + 1, :] = jnp.where(even2, to_down, to_up)
                    far_b[at : at + 1, :] = jnp.where(even2, to_up, to_down)
    blank = jnp.zeros((4, LANES), jnp.float32)
    for ref, start in ((msg_a, SLIVER + 12), (msg_b, SLIVER + 12), (far_a, 12), (far_b, 12)):
        ref[start : start + 4, :] = blank
    for ref, start in ((msg_a, RIM + 4), (msg_b, RIM + 4), (rim, 4)):
        ref[start : start + 4, :] = blank
    for ref in (mid_a, mid_b):
        ref[MAIN:MID_MSG, :] = jnp.zeros((MID_MSG - MAIN, LANES), jnp.float32)
    for k in range(2):
        turned = lanes[k * LANES : (k + 1) * LANES, :].T
        to_down = jnp.concatenate([turned[0:1], turned[127:128]], axis=0)
        to_up = jnp.concatenate([turned[1:2], turned[126:127]], axis=0)
        at = RIM + 2 * k
        msg_a[at : at + 2, :] = jnp.where(even, to_down, to_up)
        msg_b[at : at + 2, :] = jnp.where(even, to_up, to_down)
        rim[2 * k : 2 * k + 1, :] = turned[2:3]
        rim[2 * k + 1 : 2 * k + 2, :] = turned[125:126]

    for copy in edges:
        copy.wait()
    for f in range(4):
        top, bottom = (edge_f[f, 0], edge_f[f, 1]) if f < 3 else (edge_i[0], edge_i[1])
        to_up = top[0:4].astype(jnp.float32)
        to_down = bottom[4:8].astype(jnp.float32)
        first = jnp.where(even, to_down, to_up)
        second = jnp.where(even, to_up, to_down)
        for k in range(4):
            at = EDGE + (f * 4 + k) * 4
            msg_a[at : at + 4, :] = first[:, k * LANES : (k + 1) * LANES]
            msg_b[at : at + 4, :] = second[:, k * LANES : (k + 1) * LANES]


def column_kernel(
    place, own, rim, got_a, got_b, gotfar_a, gotfar_b, h_in, m_in, n_in, w_in,
    msg_a, msg_b, far_a, far_b, tail1, ring, turned_own, edges, lanes,
):
    i, j = place[0], place[1]
    even = i % 2 == 0
    even2 = (i // 2) % 2 == 0
    above_ok, below_ok = i > 0, i < SIDE - 1
    above2_ok, below2_ok = i > 1, i < SIDE - 2
    even_j = j % 2 == 0
    even2_j = (j // 2) % 2 == 0

    def from_above(rows):
        return jnp.where(even, got_b[rows, :], got_a[rows, :])

    def from_below(rows):
        return jnp.where(even, got_a[rows, :], got_b[rows, :])

    tails = []
    for b in range(3):
        rows = slice(SLIVER + 4 * b, SLIVER + 4 * b + 4)
        far = slice(4 * b, 4 * b + 4)
        above = jnp.where(above_ok, from_above(rows), 0.0)
        above = above + jnp.where(
            above2_ok, jnp.where(even2, gotfar_b[far, :], gotfar_a[far, :]), 0.0
        )
        below = jnp.where(below_ok, from_below(rows), 0.0)
        below = below + jnp.where(
            below2_ok, jnp.where(even2, gotfar_a[far, :], gotfar_b[far, :]), 0.0
        )
        tails.append(own[b, MAIN:RING, :] + jnp.concatenate([below, above], axis=0))
    tail1[...] = tails[1]

    sums = []
    for b, base in ((0, 0), (2, MAIN)):
        rows = slice(base, base + MAIN)
        main = own[b, 0:MAIN, :]
        main = main + jnp.where(above_ok, from_above(rows), 0.0)
        main = main + jnp.where(below_ok, from_below(rows), 0.0)
        sums.append(main)
    left_sum, right_sum = sums
    msg_a[0:MAIN, :] = jnp.where(even_j, right_sum, left_sum)
    msg_b[0:MAIN, :] = jnp.where(even_j, left_sum, right_sum)
    msg_a[MAIN:RING, :] = jnp.where(even_j, tails[2], tails[0])
    msg_b[MAIN:RING, :] = jnp.where(even_j, tails[0], tails[2])

    for f in range(4):
        for k in range(4):
            rows = slice(EDGE + (f * 4 + k) * 4, EDGE + (f * 4 + k) * 4 + 4)
            edges[f, :, k * LANES : (k + 1) * LANES] = jnp.concatenate(
                [from_below(rows), from_above(rows)], axis=0
            )

    def tuck(packed, lane, block, source, target, count):
        moved = pltpu.roll(block, (target - source) % LANES, 1) if target != source else block
        return jnp.where((lane >= target) & (lane < target + count), moved, packed)

    fields = (h_in, m_in, n_in, w_in)
    lane = lax.broadcasted_iota(jnp.int32, (ROWS, LANES), 1)
    packed = jnp.zeros((ROWS, LANES), jnp.float32)
    lane8 = lax.broadcasted_iota(jnp.int32, (8, LANES), 1)
    packed8 = jnp.zeros((8, LANES), jnp.float32)
    for f, field in enumerate(fields):
        right = field[:, COLS - LANES : COLS].astype(jnp.float32)
        packed = tuck(packed, lane, right, LANES - 8, 8 * f, 8)
        left = field[:, 0:LANES].astype(jnp.float32)
        packed = tuck(packed, lane, left, 0, 32 + 8 * f, 8)
        packed8 = tuck(packed8, lane8, edges[f, :, COLS - LANES : COLS], LANES - 8, 8 * f, 8)
        packed8 = tuck(packed8, lane8, edges[f, :, 0:LANES], 0, 32 + 8 * f, 8)
    spots = ((2, LANES - 1, 64), (0, 0, 65), (0, LANES - 1, 66), (2, 0, 67))
    for b, source, target in spots:
        packed = tuck(packed, lane, sums[b // 2], source, target, 1)
        packed8 = tuck(packed8, lane8, tails[b], source, target, 1)
    packed8 = tuck(packed8, lane8, tails[1], 0, 68, 1)
    packed8 = tuck(packed8, lane8, tails[1], LANES - 1, 69, 1)
    lanes[0:ROWS, :] = packed
    lanes[ROWS : ROWS + 4, :] = packed8[0:4]
    lanes[ROWS + 4 : TALL - 4, :] = jnp.zeros((TALL - ROWS - 8, LANES), jnp.float32)
    lanes[TALL - 4 : TALL, :] = packed8[4:8]

    zero8 = jnp.zeros((8, LANES), jnp.float32)
    far_a[...] = zero8
    far_b[...] = zero8
    ring[...] = zero8
    for k in range(3):
        turned = lanes[k * LANES : (k + 1) * LANES, :].T
        turned_own[k] = turned[0:64]
        if k < 2:
            rims = []
            for side in range(2):
                row = slice(RIM + 2 * k + side, RIM + 2 * k + side + 1)
                value = rim[2 * k + side : 2 * k + side + 1, :]
                value = value + jnp.where(above_ok, from_above(row), 0.0)
                rims.append(value + jnp.where(below_ok, from_below(row), 0.0))
        else:
            rims = [turned[68:69], turned[69:70]]
        to_right = [turned[8 * f + 4 : 8 * f + 8] for f in range(3)] + [rims[1], turned[29:32]]
        to_left = [turned[32 + 8 * f : 36 + 8 * f] for f in range(3)] + [turned[56:59], rims[0]]
        to_right = jnp.concatenate(to_right, axis=0)
        to_left = jnp.concatenate(to_left, axis=0)
        at = TURNED + 16 * k
        msg_a[at : at + 16, :] = jnp.where(even_j, to_right, to_left)
        msg_b[at : at + 16, :] = jnp.where(even_j, to_left, to_right)
        far_a[k : k + 1, :] = jnp.where(even2_j, turned[64:65], turned[65:66])
        far_b[k : k + 1, :] = jnp.where(even2_j, turned[65:66], turned[64:65])
        ring[k : k + 1, :] = turned[66:67]
        ring[4 + k : 5 + k, :] = turned[67:68]


def spread_matrix():
    coarse = lax.broadcasted_iota(jnp.int32, (LANES, COLS), 0)
    fine = lax.broadcasted_iota(jnp.int32, (LANES, COLS), 1)
    return jnp.where(fine // 4 == coarse, 1.0, 0.0).astype(jnp.bfloat16)


def widen(value, spread):
    part = value.astype(jnp.bfloat16)
    rest = (value - part.astype(jnp.float32)).astype(jnp.bfloat16)
    dot = functools.partial(jnp.dot, preferred_element_type=jnp.float32)
    return dot(part, spread) + dot(rest, spread)


def fluxes(height, east, north):
    inverse = 1.0 / height
    v = north * inverse
    pressure = 0.05 * height * height
    fm = 0.1 * east
    gn = 0.1 * north
    fmm = fm * (east * inverse) + pressure
    fmn = fm * v
    gnn = gn * v + pressure
    quarter = (0.25 * height, 0.25 * east, 0.25 * north)
    return quarter, (fm, fmm, fmn), (gn, fmn, gnn)


def interior_step(load, store, ready=None):
    sub = lax.broadcasted_iota(jnp.int32, (8, COLS), 0)
    first_row, last_row = sub == 0, sub == 7
    zeros = jnp.zeros((8, COLS), jnp.float32)

    def finish(at, partial, ahead):
        store(at, [p + jnp.where(last_row, u, 0.0) for p, u in zip(partial, ahead)])

    def body(c, carry):
        partial, above = carry
        at = pl.multiple_of(c * 8, 8)
        quarter, east_flux, north_flux = fluxes(*load(at))
        below = [pltpu.roll(q + x, 1, 0) for q, x in zip(quarter, east_flux)]
        ahead = [pltpu.roll(q - x, 7, 0) for q, x in zip(quarter, east_flux)]
        new_partial = [
            pltpu.roll(q - g, COLS - 1, 1)
            + pltpu.roll(q + g, 1, 1)
            + jnp.where(first_row, a, b)
            + jnp.where(last_row, 0.0, u)
            for q, g, a, b, u in zip(quarter, north_flux, above, below, ahead)
        ]
        finish(pl.multiple_of(jnp.maximum(c - 1, 0) * 8, 8), partial, ahead)
        return new_partial, below

    carry = ([zeros] * 3, [zeros] * 3)
    if ready is None:
        carry = lax.fori_loop(0, ROWS // 8, body, carry, unroll=UNROLL)
    else:
        for q in range(4):
            ready(q)
            carry = lax.fori_loop(q * 8, q * 8 + 8, body, carry, unroll=UNROLL)
    finish(ROWS - 8, carry[0], [zeros] * 3)


def first_kernel(h_in, m_in, n_in, w_in, h_near, m_near, n_near, w_near, moved, sems):
    part = ROWS // 4
    pairs = ((h_in, h_near), (m_in, m_near), (n_in, n_near))

    def fetch(pair, q, sem):
        rows = slice(q * part, q * part + part)
        return pltpu.make_async_copy(pair[0].at[rows], pair[1].at[rows], sem)

    copies = [[fetch(pair, q, sems.at[q, f]) for f, pair in enumerate(pairs)] for q in range(4)]
    mask = pltpu.make_async_copy(w_in, w_near, sems.at[4, 0])
    for q in range(4):
        for copy in copies[q]:
            copy.start()
    mask.start()

    def load(at):
        return [ref[pl.ds(at, 8), :] for ref in (h_near, m_near, n_near)]

    def store(at, values):
        for f in range(3):
            moved[f, pl.ds(at, 8), :] = values[f]

    def ready(q):
        for copy in copies[q]:
            copy.wait()

    interior_step(load, store, ready)
    mask.wait()


def main_kernel(
    place, own, mid_a, mid_b, got_a, got_b, moved, w_in,
    h_out, m_out, n_out, total, state, lift,
):
    i, j = place[0], place[1]
    even = i % 2 == 0
    even_j = j % 2 == 0
    rows = slice(0, MAIN)
    value = own[1, rows, :]
    value = value + jnp.where(i > 0, jnp.where(even, mid_b[rows, :], mid_a[rows, :]), 0.0)
    value = value + jnp.where(i < SIDE - 1, jnp.where(even, mid_a[rows, :], mid_b[rows, :]), 0.0)
    value = value + jnp.where(j > 0, jnp.where(even_j, got_b[rows, :], got_a[rows, :]), 0.0)
    value = value + jnp.where(
        j < SIDE - 1, jnp.where(even_j, got_a[rows, :], got_b[rows, :]), 0.0
    )
    total[...] = 0.05 * value
    lift[...] = widen(total[...], spread_matrix())
    upper_half = lax.broadcasted_iota(jnp.int32, (8, COLS), 0) < 4

    def source_and_mask(s, at, values):
        row = s * UX + at // 4
        raised = jnp.where(
            upper_half,
            jnp.broadcast_to(lift[pl.ds(row, 1), :], (8, COLS)),
            jnp.broadcast_to(lift[pl.ds(row + 1, 1), :], (8, COLS)),
        )
        mask = w_in[pl.ds(at, 8), :].astype(jnp.float32)
        return [values[0] + raised, values[1] * mask, values[2] * mask]

    for s in range(1, STEPS):

        def load(at, s=s):
            if s == 1:
                return source_and_mask(0, at, [moved[f, pl.ds(at, 8), :] for f in range(3)])
            return [state[s % 2, f, pl.ds(at, 8), :] for f in range(3)]

        def store(at, values, s=s):
            values = source_and_mask(s, at, values)
            for f in range(3):
                if s == STEPS - 1:
                    (h_out, m_out, n_out)[f][pl.ds(at, 8), :] = values[f]
                else:
                    state[(s + 1) % 2, f, pl.ds(at, 8), :] = values[f]

        interior_step(load, store)


def strip_kernel(
    place, total, tail1, got_a, got_b, gotfar_a, gotfar_b, ring, turned_own, edges,
    h_0, m_0, n_0, w_in, h_in, m_in, n_in, h_out, m_out, n_out, block, sides, ends, sems,
):
    inner = slice(LANES, COLS - LANES)
    copies = []
    for f, (source, target) in enumerate(((h_in, h_out), (m_in, m_out), (n_in, n_out))):
        rows = slice(8, ROWS - 8)
        copies.append(
            pltpu.make_async_copy(source.at[rows, inner], target.at[rows, inner], sems.at[0, f])
        )
        copies[f].start()

    i, j = place[0], place[1]
    even_j = j % 2 == 0
    even2_j = (j // 2) % 2 == 0
    spread = spread_matrix()

    def from_left(rows):
        return jnp.where(even_j, got_b[rows, :], got_a[rows, :])

    def from_right(rows):
        return jnp.where(even_j, got_a[rows, :], got_b[rows, :])

    tail = tail1[...] + jnp.where(j > 0, from_left(slice(MAIN, RING)), 0.0)
    tail = 0.05 * (tail + jnp.where(j < SIDE - 1, from_right(slice(MAIN, RING)), 0.0))

    def six(values):
        return jnp.concatenate([jnp.broadcast_to(v, (4, v.shape[1])) for v in values], axis=0)

    coarse = []
    for s in range(STEPS):
        at = s * UX
        coarse += [
            tail[4 + s : 5 + s], total[at : at + 2, :], total[at + UX - 2 : at + UX, :], tail[s : s + 1],
        ]
    fine = widen(jnp.concatenate(coarse, axis=0), spread)
    row_lift = [
        six([fine[6 * s + r : 6 * s + r + 1] for r in range(6)]) for s in range(STEPS)
    ]
    row_state = []
    for f, field in enumerate((h_0, m_0, n_0, w_in)):
        row_state.append(
            jnp.concatenate(
                [
                    edges[f, 4:8, :],
                    field[0:8, :].astype(jnp.float32),
                    field[ROWS - 8 : ROWS, :].astype(jnp.float32),
                    edges[f, 0:4, :],
                ],
                axis=0,
            )
        )

    parts = [[], [], [], []]
    ups = []
    for k in range(3):
        at = TURNED + 16 * k
        left, right = from_left(slice(at, at + 16)), from_right(slice(at, at + 16))
        for f in range(4):
            parts[f].append(
                jnp.concatenate(
                    [
                        left[4 * f : 4 * f + 4],
                        turned_own[k, 32 + 8 * f : 40 + 8 * f, :],
                        turned_own[k, 8 * f : 8 * f + 8, :],
                        right[4 * f : 4 * f + 4],
                    ],
                    axis=0,
                )
            )
        far_left = jnp.where(even2_j, gotfar_b[k : k + 1, :], gotfar_a[k : k + 1, :])
        far_right = jnp.where(even2_j, gotfar_a[k : k + 1, :], gotfar_b[k : k + 1, :])
        ring_left = ring[k : k + 1, :] + left[12:13] + jnp.where(j > 1, far_left, 0.0)
        ring_right = ring[4 + k : 5 + k, :] + right[15:16]
        ring_right = ring_right + jnp.where(j < SIDE - 2, far_right, 0.0)
        if k < 2:
            turned = total[k * LANES : (k + 1) * LANES, :].T
        else:
            block[...] = jnp.zeros((LANES, LANES), jnp.float32)
            block[0:4, :] = tail[0:4]
            block[LANES - 4 : LANES, :] = tail[4:8]
            turned = block[...].T
        ups.append(
            jnp.concatenate(
                [0.05 * ring_left, turned[0:2], turned[126:128], 0.05 * ring_right, turned[0:2]],
                axis=0,
            )
        )
    col_state = [jnp.concatenate(p, axis=1) for p in parts]
    lane = lax.broadcasted_iota(jnp.int32, (8, LANES), 1)
    col_lift = []
    for s in range(STEPS):
        if s % 2 == 0:
            wide = widen(ups[s // 2], spread)
        own_rows = wide[:, 256 * (s % 2) : 256 * (s % 2) + 256]
        beside = jnp.where(
            lane < 4,
            jnp.broadcast_to(ups[2][:, s : s + 1], (8, LANES)),
            jnp.broadcast_to(ups[2][:, LANES - 4 + s : LANES - 3 + s], (8, LANES)),
        )
        both = jnp.concatenate([own_rows, beside], axis=1)
        col_lift.append(six([both[r : r + 1] for r in range(6)]))

    def advance(state, lift, wet, x_axis, ends):
        n_sub, n_lane = state[0].shape
        sub = lax.broadcasted_iota(jnp.int32, (n_sub, n_lane), 0)
        lanes = lax.broadcasted_iota(jnp.int32, (n_sub, n_lane), 1)
        fixed = []
        for value in state:
            value = jnp.where((sub == 3) & ends[0], pltpu.roll(value, n_sub - 1, 0), value)
            value = jnp.where((sub == 20) & ends[1], pltpu.roll(value, 1, 0), value)
            if len(ends) == 4:
                blocks = [value[:, k * LANES : (k + 1) * LANES] for k in range(3)]
                last = lanes[:, 0:LANES] == LANES - 1
                blocks[2] = jnp.where(last & ends[2], pltpu.roll(blocks[0], LANES - 1, 1), blocks[2])
                initial = lanes[:, 0:LANES] == 0
                blocks[2] = jnp.where(initial & ends[3], pltpu.roll(blocks[1], 1, 1), blocks[2])
                value = jnp.concatenate(blocks, axis=1)
            fixed.append(value)
        quarter, east_flux, north_flux = fluxes(*fixed)
        along_sub, along_lane = (east_flux, north_flux) if x_axis == 0 else (north_flux, east_flux)
        out = [
            pltpu.roll(q - a, n_sub - 1, 0)
            + pltpu.roll(q + a, 1, 0)
            + pltpu.roll(q - l, n_lane - 1, 1)
            + pltpu.roll(q + l, 1, 1)
            for q, a, l in zip(quarter, along_sub, along_lane)
        ]
        return [out[0] + lift, out[1] * wet, out[2] * wet]

    row_ends = (i == 0, i == SIDE - 1)
    col_ends = (j == 0, j == SIDE - 1) + row_ends
    rows, cols = row_state[:3], col_state[:3]
    for s in range(STEPS):
        rows = advance(rows, row_lift[s], row_state[3], 0, row_ends)
        cols = advance(cols, col_lift[s], col_state[3], 1, col_ends)

    lane = lax.broadcasted_iota(jnp.int32, (ROWS, LANES), 1)
    for f in range(3):
        block[8 * f : 8 * f + 4, :] = cols[f][16:20, 0:LANES]
        block[8 * f + 4 : 8 * f + 8, :] = cols[f][4:8, 0:LANES]
    upper = block[...].T
    for f in range(3):
        block[8 * f : 8 * f + 4, :] = cols[f][16:20, LANES : 2 * LANES]
        block[8 * f + 4 : 8 * f + 8, :] = cols[f][4:8, LANES : 2 * LANES]
    rim = jnp.concatenate([upper, block[...].T], axis=0)
    for f, (source, target) in enumerate(((h_in, h_out), (m_in, m_out), (n_in, n_out))):
        side = pltpu.roll(rim, (LANES - 4 - 8 * f) % LANES, 1)
        top = jnp.concatenate([rows[f][4:8], source[4:8, :]], axis=0)
        bottom = jnp.concatenate([source[ROWS - 8 : ROWS - 4, :], rows[f][16:20]], axis=0)
        for t, (at, mine) in enumerate(((0, lane < 4), (COLS - LANES, lane >= LANES - 4))):
            part = slice(at, at + LANES)
            value = jnp.concatenate(
                [top[:, part], source[8 : ROWS - 8, part], bottom[:, part]], axis=0
            )
            sides[f, t] = jnp.where(mine, side, value)
            copies.append(
                pltpu.make_async_copy(sides.at[f, t], target.at[:, part], sems.at[1 + t, f])
            )
        for t, (at, value) in enumerate(((0, top), (ROWS - 8, bottom))):
            ends[f, t] = value[:, inner]
            copies.append(
                pltpu.make_async_copy(ends.at[f, t], target.at[at : at + 8, inner], sems.at[3 + t, f])
            )
        for copy in copies[-4:]:
            copy.start()
    for copy in copies:
        copy.wait()


def f32(*shape):
    return jax.ShapeDtypeStruct(shape, jnp.float32)


SMEM = pl.BlockSpec(memory_space=pltpu.SMEM)
VMEM = pl.BlockSpec(memory_space=pltpu.VMEM)
HBM = pl.BlockSpec(memory_space=pltpu.HBM)


def run(body, outs, in_specs, scratch, args, name, cost=None, out_spec=VMEM):
    if cost is not None:
        cost = pl.CostEstimate(flops=cost, bytes_accessed=0, transcendentals=0)
    return pl.pallas_call(
        body,
        in_specs=in_specs,
        out_specs=[out_spec] * len(outs),
        out_shape=outs,
        scratch_shapes=scratch,
        compiler_params=pltpu.CompilerParams(vmem_limit_bytes=VMEM_LIMIT),
        cost_estimate=cost,
        name=name,
    )(*args)


def shards(slip_rate, green_kernel, intersection, wet_mask, column_height, east_flow, north_flow):
    place = jnp.stack([lax.axis_index("ox"), lax.axis_index("oy")]).astype(jnp.int32)
    fields = (column_height, east_flow, north_flow, wet_mask)

    msg_a, msg_b, mid_a, mid_b, far_a, far_b, own, rim = run(
        slip_kernel,
        [f32(ROW_MSG, LANES)] * 2 + [f32(MID_MSG, LANES)] * 2 + [f32(16, LANES)] * 2
        + [f32(3, RING, LANES), f32(8, LANES)],
        [SMEM] + [HBM] * 7,
        [
            pltpu.VMEM((9, 32, UX * LANES), jnp.bfloat16),
            pltpu.SMEM((1, 9), jnp.int32),
            pltpu.VMEM((STEPS, 32), jnp.bfloat16),
            pltpu.VMEM((3, 2, 8, COLS), jnp.float32),
            pltpu.VMEM((2, 8, COLS), jnp.int32),
            pltpu.VMEM((MAIN, LANES), jnp.float32),
            pltpu.SemaphoreType.DMA((19,)),
        ],
        (place,)
        + tuple(
            pltpu.with_memory_space_constraint(x, pltpu.HBM)
            for x in (intersection, slip_rate, jnp.transpose(green_kernel, (1, 0, 2))) + fields
        ),
        "slip",
    )
    got_a = swap(msg_a, "ox", 0)
    got_b = swap(msg_b, "ox", 1)
    gotfar_a = swap(far_a, "ox", 0, 2)
    gotfar_b = swap(far_b, "ox", 1, 2)
    mid_a = swap(mid_a, "ox", 0)
    mid_b = swap(mid_b, "ox", 1)

    *near, moved = run(
        first_kernel,
        [f32(ROWS, COLS)] * 3 + [jax.ShapeDtypeStruct((ROWS, COLS), jnp.int32), f32(3, ROWS, COLS)],
        [HBM] * 4,
        [pltpu.SemaphoreType.DMA((5, 3))],
        [pltpu.with_memory_space_constraint(x, pltpu.HBM) for x in fields],
        "first",
    )
    near = tuple(near)
    msg_a, msg_b, far_a, far_b, tail1, ring, turned_own, edges = run(
        column_kernel,
        [f32(COL_MSG, LANES)] * 2 + [f32(8, LANES)] * 4 + [f32(3, 64, LANES), f32(4, 8, COLS)],
        [SMEM] + [VMEM] * 10,
        [pltpu.VMEM((TALL, LANES), jnp.float32)],
        (place, own, rim, got_a, got_b, gotfar_a, gotfar_b) + near,
        "column",
        10**10,
    )
    got_a = swap(msg_a, "oy", 0)
    got_b = swap(msg_b, "oy", 1)
    gotfar_a = swap(far_a, "oy", 0, 2)
    gotfar_b = swap(far_b, "oy", 1, 2)

    height, east, north, total = run(
        main_kernel,
        [f32(ROWS, COLS)] * 3 + [f32(MAIN, LANES)],
        [SMEM] + [VMEM] * 7,
        [
            pltpu.VMEM((2, 3, ROWS, COLS), jnp.float32),
            pltpu.VMEM((MAIN, COLS), jnp.float32),
        ],
        (place, own, mid_a, mid_b, got_a, got_b, moved, near[3]),
        "main",
        10**10,
    )
    return tuple(
        run(
            strip_kernel,
            [f32(ROWS, COLS)] * 3,
            [SMEM] + [VMEM] * 16,
            [
                pltpu.VMEM((LANES, LANES), jnp.float32),
                pltpu.VMEM((3, 2, ROWS, LANES), jnp.float32),
                pltpu.VMEM((3, 2, 8, COLS - 2 * LANES), jnp.float32),
                pltpu.SemaphoreType.DMA((5, 3)),
            ],
            (place, total, tail1, got_a, got_b, gotfar_a, gotfar_b, ring, turned_own, edges)
            + near + (height, east, north),
            "strip",
            out_spec=HBM,
        )
    )


def solution(mesh):
    return jax.shard_map(
        shards,
        mesh=mesh,
        in_specs=(
            P(None, ("ox", "oy")),
            P(("ox", "oy"), None, None),
            P(("ox", "oy"), None),
            P("ox", "oy"),
            P("ox", "oy"),
            P("ox", "oy"),
            P("ox", "oy"),
        ),
        out_specs=(P("ox", "oy"), P("ox", "oy"), P("ox", "oy")),
        check_vma=False,
    )
```

```python
import functools

import jax
import jax.numpy as jnp
from jax import lax
from jax.experimental import pallas as pl
from jax.experimental.pallas import tpu as pltpu
from jax.sharding import PartitionSpec as P

STEPS = 4
SIDE = 16
ROWS = 256
COLS = 512
LANES = 128
UX = 64
MAIN = STEPS * UX
RING = MAIN + 8
SLIVER = 2 * MAIN
EDGE = SLIVER + 16
RIM = EDGE + 64
ROW_MSG = RIM + 8
TURNED = RING
COL_MSG = RING + 48
MID_MSG = COL_MSG + 8
TALL = 3 * LANES
UNROLL = 16
VMEM_LIMIT = 24 * 1024 * 1024


def partners(axis, parity, reach):
    return [
        (i, (i + reach if (i // reach) % 2 == parity else i - reach) % SIDE)
        for i in range(SIDE)
    ]


def swap(value, axis, parity, reach=1):
    return lax.ppermute(value, axis, partners(axis, parity, reach))


def slip_kernel(
    place, cover_in, slip_in, green, h_in, m_in, n_in, w_in,
    msg_a, msg_b, mid_a, mid_b, far_a, far_b, own, rim, held, cover, slip, edge_f, edge_i, lanes, sems,
):
    def fetch(slot):
        return pltpu.make_async_copy(green.at[slot], held.at[slot], sems.at[slot])

    small = [
        pltpu.make_async_copy(slip_in, slip, sems.at[9]),
        pltpu.make_async_copy(cover_in, cover, sems.at[10]),
    ]
    edges = []
    for f, field in enumerate((h_in, m_in, n_in, w_in)):
        for t, start in enumerate((0, ROWS - 8)):
            target = edge_f.at[f, t] if f < 3 else edge_i.at[t]
            edges.append(
                pltpu.make_async_copy(field.at[start : start + 8], target, sems.at[11 + 2 * f + t])
            )
    for copy in small:
        copy.start()
    order = (0, 6, 3, 1, 7, 4, 2, 8, 5)
    for slot in order:
        fetch(slot).start()
    for copy in edges:
        copy.start()
    for copy in small:
        copy.wait()
    even = place[0] % 2 == 0
    even2 = (place[0] // 2) % 2 == 0

    rates = slip[...].astype(jnp.float32)
    rates = jnp.concatenate([rates] * 8, axis=1)
    rates = jnp.concatenate(
        [jnp.broadcast_to(rates[s : s + 1], (8, 256)) for s in range(STEPS)], axis=0
    )
    row = lax.broadcasted_iota(jnp.int32, (32, 256), 0)
    col = lax.broadcasted_iota(jnp.int32, (32, 256), 1)
    spread = jnp.where(col // 32 == row % 8, rates, 0.0).astype(jnp.bfloat16)
    lane = lax.broadcasted_iota(jnp.int32, (32, LANES), 1)

    def group(slot, g):
        right = jnp.concatenate(
            [held[slot, :, (g * 8 + p) * LANES : (g * 8 + p + 1) * LANES] for p in range(8)],
            axis=0,
        )
        value = jnp.dot(spread, right, preferred_element_type=jnp.float32)
        return value * cover[0, slot].astype(jnp.float32)

    def rims(down, up, mid):
        value = jnp.where(lane == 1, pltpu.roll(up, 1, 1), down)
        value = jnp.where(lane == LANES - 2, pltpu.roll(up, LANES - 1, 1), value)
        value = jnp.where(lane == 2, pltpu.roll(mid, 2, 1), value)
        return jnp.where(lane == LANES - 3, pltpu.roll(mid, LANES - 2, 1), value)

    for b in range(3):
        fetch(b).wait()
        fetch(6 + b).wait()
        fetch(3 + b).wait()
        to_a, to_b, base = ((msg_a, msg_b, 0), (mid_a, mid_b, 0), (msg_a, msg_b, MAIN))[b]
        for g in range(8):
            up = group(b, g)
            down = group(6 + b, g)
            mid = group(3 + b, g)
            first = jnp.where(even, down, up)
            second = jnp.where(even, up, down)
            if b == 1:
                rim_lanes = rims(down, up, mid)
            for s in range(STEPS):
                part = slice(8 * s, 8 * s + 8)
                at = s * UX + g * 8
                to_a[base + at : base + at + 8, :] = first[part]
                to_b[base + at : base + at + 8, :] = second[part]
                own[b, at : at + 8, :] = mid[part]
                if b == 1:
                    lanes[at : at + 8, :] = rim_lanes[part]
            if g == 0:
                for s in range(STEPS):
                    own[b, MAIN + s : MAIN + s + 1, :] = down[8 * s : 8 * s + 1]
                up_edge, up_mid = up, mid
            if g == 7:
                for s in range(STEPS):
                    own[b, MAIN + 4 + s : MAIN + 5 + s, :] = up[8 * s + 7 : 8 * s + 8]
                    at = b * STEPS + s
                    to_down = mid[8 * s + 7 : 8 * s + 8]
                    to_up = up_mid[8 * s : 8 * s + 1]
                    msg_a[SLIVER + at : SLIVER + at + 1, :] = jnp.where(even, to_down, to_up)
                    msg_b[SLIVER + at : SLIVER + at + 1, :] = jnp.where(even, to_up, to_down)
                    to_down = down[8 * s + 7 : 8 * s + 8]
                    to_up = up_edge[8 * s : 8 * s + 1]
                    far_a[at : at + 1, :] = jnp.where(even2, to_down, to_up)
                    far_b[at : at + 1, :] = jnp.where(even2, to_up, to_down)
    blank = jnp.zeros((4, LANES), jnp.float32)
    for ref, start in ((msg_a, SLIVER + 12), (msg_b, SLIVER + 12), (far_a, 12), (far_b, 12)):
        ref[start : start + 4, :] = blank
    for ref, start in ((msg_a, RIM + 4), (msg_b, RIM + 4), (rim, 4)):
        ref[start : start + 4, :] = blank
    for ref in (mid_a, mid_b):
        ref[MAIN:MID_MSG, :] = jnp.zeros((MID_MSG - MAIN, LANES), jnp.float32)
    for k in range(2):
        turned = lanes[k * LANES : (k + 1) * LANES, :].T
        to_down = jnp.concatenate([turned[0:1], turned[127:128]], axis=0)
        to_up = jnp.concatenate([turned[1:2], turned[126:127]], axis=0)
        at = RIM + 2 * k
        msg_a[at : at + 2, :] = jnp.where(even, to_down, to_up)
        msg_b[at : at + 2, :] = jnp.where(even, to_up, to_down)
        rim[2 * k : 2 * k + 1, :] = turned[2:3]
        rim[2 * k + 1 : 2 * k + 2, :] = turned[125:126]

    for copy in edges:
        copy.wait()
    for f in range(4):
        top, bottom = (edge_f[f, 0], edge_f[f, 1]) if f < 3 else (edge_i[0], edge_i[1])
        to_up = top[0:4].astype(jnp.float32)
        to_down = bottom[4:8].astype(jnp.float32)
        first = jnp.where(even, to_down, to_up)
        second = jnp.where(even, to_up, to_down)
        for k in range(4):
            at = EDGE + (f * 4 + k) * 4
            msg_a[at : at + 4, :] = first[:, k * LANES : (k + 1) * LANES]
            msg_b[at : at + 4, :] = second[:, k * LANES : (k + 1) * LANES]


def column_kernel(
    place, own, rim, got_a, got_b, gotfar_a, gotfar_b, h_in, m_in, n_in, w_in,
    msg_a, msg_b, far_a, far_b, tail1, ring, turned_own, edges, lanes,
):
    i, j = place[0], place[1]
    even = i % 2 == 0
    even2 = (i // 2) % 2 == 0
    above_ok, below_ok = i > 0, i < SIDE - 1
    above2_ok, below2_ok = i > 1, i < SIDE - 2
    even_j = j % 2 == 0
    even2_j = (j // 2) % 2 == 0

    def from_above(rows):
        return jnp.where(even, got_b[rows, :], got_a[rows, :])

    def from_below(rows):
        return jnp.where(even, got_a[rows, :], got_b[rows, :])

    tails = []
    for b in range(3):
        rows = slice(SLIVER + 4 * b, SLIVER + 4 * b + 4)
        far = slice(4 * b, 4 * b + 4)
        above = jnp.where(above_ok, from_above(rows), 0.0)
        above = above + jnp.where(
            above2_ok, jnp.where(even2, gotfar_b[far, :], gotfar_a[far, :]), 0.0
        )
        below = jnp.where(below_ok, from_below(rows), 0.0)
        below = below + jnp.where(
            below2_ok, jnp.where(even2, gotfar_a[far, :], gotfar_b[far, :]), 0.0
        )
        tails.append(own[b, MAIN:RING, :] + jnp.concatenate([below, above], axis=0))
    tail1[...] = tails[1]

    sums = []
    for b, base in ((0, 0), (2, MAIN)):
        rows = slice(base, base + MAIN)
        main = own[b, 0:MAIN, :]
        main = main + jnp.where(above_ok, from_above(rows), 0.0)
        main = main + jnp.where(below_ok, from_below(rows), 0.0)
        sums.append(main)
    left_sum, right_sum = sums
    msg_a[0:MAIN, :] = jnp.where(even_j, right_sum, left_sum)
    msg_b[0:MAIN, :] = jnp.where(even_j, left_sum, right_sum)
    msg_a[MAIN:RING, :] = jnp.where(even_j, tails[2], tails[0])
    msg_b[MAIN:RING, :] = jnp.where(even_j, tails[0], tails[2])

    for f in range(4):
        for k in range(4):
            rows = slice(EDGE + (f * 4 + k) * 4, EDGE + (f * 4 + k) * 4 + 4)
            edges[f, :, k * LANES : (k + 1) * LANES] = jnp.concatenate(
                [from_below(rows), from_above(rows)], axis=0
            )

    def tuck(packed, lane, block, source, target, count):
        moved = pltpu.roll(block, (target - source) % LANES, 1) if target != source else block
        return jnp.where((lane >= target) & (lane < target + count), moved, packed)

    fields = (h_in, m_in, n_in, w_in)
    lane = lax.broadcasted_iota(jnp.int32, (ROWS, LANES), 1)
    packed = jnp.zeros((ROWS, LANES), jnp.float32)
    lane8 = lax.broadcasted_iota(jnp.int32, (8, LANES), 1)
    packed8 = jnp.zeros((8, LANES), jnp.float32)
    for f, field in enumerate(fields):
        right = field[:, COLS - LANES : COLS].astype(jnp.float32)
        packed = tuck(packed, lane, right, LANES - 8, 8 * f, 8)
        left = field[:, 0:LANES].astype(jnp.float32)
        packed = tuck(packed, lane, left, 0, 32 + 8 * f, 8)
        packed8 = tuck(packed8, lane8, edges[f, :, COLS - LANES : COLS], LANES - 8, 8 * f, 8)
        packed8 = tuck(packed8, lane8, edges[f, :, 0:LANES], 0, 32 + 8 * f, 8)
    spots = ((2, LANES - 1, 64), (0, 0, 65), (0, LANES - 1, 66), (2, 0, 67))
    for b, source, target in spots:
        packed = tuck(packed, lane, sums[b // 2], source, target, 1)
        packed8 = tuck(packed8, lane8, tails[b], source, target, 1)
    packed8 = tuck(packed8, lane8, tails[1], 0, 68, 1)
    packed8 = tuck(packed8, lane8, tails[1], LANES - 1, 69, 1)
    lanes[0:ROWS, :] = packed
    lanes[ROWS : ROWS + 4, :] = packed8[0:4]
    lanes[ROWS + 4 : TALL - 4, :] = jnp.zeros((TALL - ROWS - 8, LANES), jnp.float32)
    lanes[TALL - 4 : TALL, :] = packed8[4:8]

    zero8 = jnp.zeros((8, LANES), jnp.float32)
    far_a[...] = zero8
    far_b[...] = zero8
    ring[...] = zero8
    for k in range(3):
        turned = lanes[k * LANES : (k + 1) * LANES, :].T
        turned_own[k] = turned[0:64]
        if k < 2:
            rims = []
            for side in range(2):
                row = slice(RIM + 2 * k + side, RIM + 2 * k + side + 1)
                value = rim[2 * k + side : 2 * k + side + 1, :]
                value = value + jnp.where(above_ok, from_above(row), 0.0)
                rims.append(value + jnp.where(below_ok, from_below(row), 0.0))
        else:
            rims = [turned[68:69], turned[69:70]]
        to_right = [turned[8 * f + 4 : 8 * f + 8] for f in range(3)] + [rims[1], turned[29:32]]
        to_left = [turned[32 + 8 * f : 36 + 8 * f] for f in range(3)] + [turned[56:59], rims[0]]
        to_right = jnp.concatenate(to_right, axis=0)
        to_left = jnp.concatenate(to_left, axis=0)
        at = TURNED + 16 * k
        msg_a[at : at + 16, :] = jnp.where(even_j, to_right, to_left)
        msg_b[at : at + 16, :] = jnp.where(even_j, to_left, to_right)
        far_a[k : k + 1, :] = jnp.where(even2_j, turned[64:65], turned[65:66])
        far_b[k : k + 1, :] = jnp.where(even2_j, turned[65:66], turned[64:65])
        ring[k : k + 1, :] = turned[66:67]
        ring[4 + k : 5 + k, :] = turned[67:68]


def spread_matrix():
    coarse = lax.broadcasted_iota(jnp.int32, (LANES, COLS), 0)
    fine = lax.broadcasted_iota(jnp.int32, (LANES, COLS), 1)
    return jnp.where(fine // 4 == coarse, 1.0, 0.0).astype(jnp.bfloat16)


def widen(value, spread):
    part = value.astype(jnp.bfloat16)
    rest = (value - part.astype(jnp.float32)).astype(jnp.bfloat16)
    dot = functools.partial(jnp.dot, preferred_element_type=jnp.float32)
    return dot(part, spread) + dot(rest, spread)


def fluxes(height, east, north):
    inverse = 1.0 / height
    v = north * inverse
    pressure = 0.05 * height * height
    fm = 0.1 * east
    gn = 0.1 * north
    fmm = fm * (east * inverse) + pressure
    fmn = fm * v
    gnn = gn * v + pressure
    quarter = (0.25 * height, 0.25 * east, 0.25 * north)
    return quarter, (fm, fmm, fmn), (gn, fmn, gnn)


def interior_step(load, store, ready=None):
    sub = lax.broadcasted_iota(jnp.int32, (8, COLS), 0)
    first_row, last_row = sub == 0, sub == 7
    zeros = jnp.zeros((8, COLS), jnp.float32)

    def finish(at, partial, ahead, beyond):
        store(at, [p + jnp.where(last_row, b, a) for p, a, b in zip(partial, ahead, beyond)])

    def body(c, carry):
        partial, above, before = carry
        at = pl.multiple_of(c * 8, 8)
        quarter, east_flux, north_flux = fluxes(*load(at))
        below = [pltpu.roll(q + x, 1, 0) for q, x in zip(quarter, east_flux)]
        ahead = [pltpu.roll(q - x, 7, 0) for q, x in zip(quarter, east_flux)]
        new_partial = [
            pltpu.roll(q - g, COLS - 1, 1)
            + pltpu.roll(q + g, 1, 1)
            + jnp.where(first_row, a, b)
            for q, g, a, b in zip(quarter, north_flux, above, below)
        ]
        finish(pl.multiple_of(jnp.maximum(c - 1, 0) * 8, 8), partial, before, ahead)
        return new_partial, below, ahead

    carry = ([zeros] * 3, [zeros] * 3, [zeros] * 3)
    if ready is None:
        carry = lax.fori_loop(0, ROWS // 8, body, carry, unroll=UNROLL)
    else:
        for q in range(4):
            ready(q)
            carry = lax.fori_loop(q * 8, q * 8 + 8, body, carry, unroll=8)
    finish(ROWS - 8, carry[0], carry[2], carry[2])


def first_kernel(h_in, m_in, n_in, w_in, h_near, m_near, n_near, w_near, moved, sems):
    part = ROWS // 4
    pairs = ((h_in, h_near), (m_in, m_near), (n_in, n_near))

    def fetch(pair, q, sem):
        rows = slice(q * part, q * part + part)
        return pltpu.make_async_copy(pair[0].at[rows], pair[1].at[rows], sem)

    copies = [[fetch(pair, q, sems.at[q, f]) for f, pair in enumerate(pairs)] for q in range(4)]
    mask = pltpu.make_async_copy(w_in, w_near, sems.at[4, 0])
    for q in range(4):
        for copy in copies[q]:
            copy.start()
    mask.start()

    def load(at):
        return [ref[pl.ds(at, 8), :] for ref in (h_near, m_near, n_near)]

    def store(at, values):
        for f in range(3):
            moved[f, pl.ds(at, 8), :] = values[f]

    def ready(q):
        for copy in copies[q]:
            copy.wait()

    interior_step(load, store, ready)
    mask.wait()


def main_kernel(
    place, own, mid_a, mid_b, got_a, got_b, moved, w_in,
    h_out, m_out, n_out, total, state, lift,
):
    i, j = place[0], place[1]
    even = i % 2 == 0
    even_j = j % 2 == 0
    rows = slice(0, MAIN)
    value = own[1, rows, :]
    value = value + jnp.where(i > 0, jnp.where(even, mid_b[rows, :], mid_a[rows, :]), 0.0)
    value = value + jnp.where(i < SIDE - 1, jnp.where(even, mid_a[rows, :], mid_b[rows, :]), 0.0)
    value = value + jnp.where(j > 0, jnp.where(even_j, got_b[rows, :], got_a[rows, :]), 0.0)
    value = value + jnp.where(
        j < SIDE - 1, jnp.where(even_j, got_a[rows, :], got_b[rows, :]), 0.0
    )
    total[...] = 0.05 * value
    lift[...] = widen(total[...], spread_matrix())
    upper_half = lax.broadcasted_iota(jnp.int32, (8, COLS), 0) < 4

    def source_and_mask(s, at, values):
        row = s * UX + at // 4
        raised = jnp.where(
            upper_half,
            jnp.broadcast_to(lift[pl.ds(row, 1), :], (8, COLS)),
            jnp.broadcast_to(lift[pl.ds(row + 1, 1), :], (8, COLS)),
        )
        mask = w_in[pl.ds(at, 8), :].astype(jnp.float32)
        return [values[0] + raised, values[1] * mask, values[2] * mask]

    for s in range(1, STEPS):

        def load(at, s=s):
            if s == 1:
                return source_and_mask(0, at, [moved[f, pl.ds(at, 8), :] for f in range(3)])
            return [state[s % 2, f, pl.ds(at, 8), :] for f in range(3)]

        def store(at, values, s=s):
            values = source_and_mask(s, at, values)
            for f in range(3):
                if s == STEPS - 1:
                    (h_out, m_out, n_out)[f][pl.ds(at, 8), :] = values[f]
                else:
                    state[(s + 1) % 2, f, pl.ds(at, 8), :] = values[f]

        interior_step(load, store)


def strip_kernel(
    place, total, tail1, got_a, got_b, gotfar_a, gotfar_b, ring, turned_own, edges,
    h_0, m_0, n_0, w_in, h_in, m_in, n_in, h_out, m_out, n_out, block, sides, ends, sems,
):
    inner = slice(LANES, COLS - LANES)
    copies = []
    for f, (source, target) in enumerate(((h_in, h_out), (m_in, m_out), (n_in, n_out))):
        rows = slice(8, ROWS - 8)
        copies.append(
            pltpu.make_async_copy(source.at[rows, inner], target.at[rows, inner], sems.at[0, f])
        )
        copies[f].start()

    i, j = place[0], place[1]
    even_j = j % 2 == 0
    even2_j = (j // 2) % 2 == 0
    spread = spread_matrix()

    def from_left(rows):
        return jnp.where(even_j, got_b[rows, :], got_a[rows, :])

    def from_right(rows):
        return jnp.where(even_j, got_a[rows, :], got_b[rows, :])

    tail = tail1[...] + jnp.where(j > 0, from_left(slice(MAIN, RING)), 0.0)
    tail = 0.05 * (tail + jnp.where(j < SIDE - 1, from_right(slice(MAIN, RING)), 0.0))

    def six(values):
        return jnp.concatenate([jnp.broadcast_to(v, (4, v.shape[1])) for v in values], axis=0)

    coarse = []
    for s in range(STEPS):
        at = s * UX
        coarse += [
            tail[4 + s : 5 + s], total[at : at + 2, :], total[at + UX - 2 : at + UX, :], tail[s : s + 1],
        ]
    fine = widen(jnp.concatenate(coarse, axis=0), spread)
    row_lift = [
        six([fine[6 * s + r : 6 * s + r + 1] for r in range(6)]) for s in range(STEPS)
    ]
    row_state = []
    for f, field in enumerate((h_0, m_0, n_0, w_in)):
        row_state.append(
            jnp.concatenate(
                [
                    edges[f, 4:8, :],
                    field[0:8, :].astype(jnp.float32),
                    field[ROWS - 8 : ROWS, :].astype(jnp.float32),
                    edges[f, 0:4, :],
                ],
                axis=0,
            )
        )

    parts = [[], [], [], []]
    ups = []
    for k in range(3):
        at = TURNED + 16 * k
        left, right = from_left(slice(at, at + 16)), from_right(slice(at, at + 16))
        for f in range(4):
            parts[f].append(
                jnp.concatenate(
                    [
                        left[4 * f : 4 * f + 4],
                        turned_own[k, 32 + 8 * f : 40 + 8 * f, :],
                        turned_own[k, 8 * f : 8 * f + 8, :],
                        right[4 * f : 4 * f + 4],
                    ],
                    axis=0,
                )
            )
        far_left = jnp.where(even2_j, gotfar_b[k : k + 1, :], gotfar_a[k : k + 1, :])
        far_right = jnp.where(even2_j, gotfar_a[k : k + 1, :], gotfar_b[k : k + 1, :])
        ring_left = ring[k : k + 1, :] + left[12:13] + jnp.where(j > 1, far_left, 0.0)
        ring_right = ring[4 + k : 5 + k, :] + right[15:16]
        ring_right = ring_right + jnp.where(j < SIDE - 2, far_right, 0.0)
        if k < 2:
            turned = total[k * LANES : (k + 1) * LANES, :].T
        else:
            block[...] = jnp.zeros((LANES, LANES), jnp.float32)
            block[0:4, :] = tail[0:4]
            block[LANES - 4 : LANES, :] = tail[4:8]
            turned = block[...].T
        ups.append(
            jnp.concatenate(
                [0.05 * ring_left, turned[0:2], turned[126:128], 0.05 * ring_right, turned[0:2]],
                axis=0,
            )
        )
    col_state = [jnp.concatenate(p, axis=1) for p in parts]
    lane = lax.broadcasted_iota(jnp.int32, (8, LANES), 1)
    col_lift = []
    for s in range(STEPS):
        if s % 2 == 0:
            wide = widen(ups[s // 2], spread)
        own_rows = wide[:, 256 * (s % 2) : 256 * (s % 2) + 256]
        beside = jnp.where(
            lane < 4,
            jnp.broadcast_to(ups[2][:, s : s + 1], (8, LANES)),
            jnp.broadcast_to(ups[2][:, LANES - 4 + s : LANES - 3 + s], (8, LANES)),
        )
        both = jnp.concatenate([own_rows, beside], axis=1)
        col_lift.append(six([both[r : r + 1] for r in range(6)]))

    def advance(state, lift, wet, x_axis, ends):
        n_sub, n_lane = state[0].shape
        sub = lax.broadcasted_iota(jnp.int32, (n_sub, n_lane), 0)
        lanes = lax.broadcasted_iota(jnp.int32, (n_sub, n_lane), 1)
        fixed = []
        for value in state:
            value = jnp.where((sub == 3) & ends[0], pltpu.roll(value, n_sub - 1, 0), value)
            value = jnp.where((sub == 20) & ends[1], pltpu.roll(value, 1, 0), value)
            if len(ends) == 4:
                blocks = [value[:, k * LANES : (k + 1) * LANES] for k in range(3)]
                last = lanes[:, 0:LANES] == LANES - 1
                blocks[2] = jnp.where(last & ends[2], pltpu.roll(blocks[0], LANES - 1, 1), blocks[2])
                initial = lanes[:, 0:LANES] == 0
                blocks[2] = jnp.where(initial & ends[3], pltpu.roll(blocks[1], 1, 1), blocks[2])
                value = jnp.concatenate(blocks, axis=1)
            fixed.append(value)
        quarter, east_flux, north_flux = fluxes(*fixed)
        along_sub, along_lane = (east_flux, north_flux) if x_axis == 0 else (north_flux, east_flux)
        out = [
            pltpu.roll(q - a, n_sub - 1, 0)
            + pltpu.roll(q + a, 1, 0)
            + pltpu.roll(q - l, n_lane - 1, 1)
            + pltpu.roll(q + l, 1, 1)
            for q, a, l in zip(quarter, along_sub, along_lane)
        ]
        return [out[0] + lift, out[1] * wet, out[2] * wet]

    row_ends = (i == 0, i == SIDE - 1)
    col_ends = (j == 0, j == SIDE - 1) + row_ends
    rows, cols = row_state[:3], col_state[:3]
    for s in range(STEPS):
        rows = advance(rows, row_lift[s], row_state[3], 0, row_ends)
        cols = advance(cols, col_lift[s], col_state[3], 1, col_ends)

    lane = lax.broadcasted_iota(jnp.int32, (ROWS, LANES), 1)
    for f in range(3):
        block[8 * f : 8 * f + 4, :] = cols[f][16:20, 0:LANES]
        block[8 * f + 4 : 8 * f + 8, :] = cols[f][4:8, 0:LANES]
    upper = block[...].T
    for f in range(3):
        block[8 * f : 8 * f + 4, :] = cols[f][16:20, LANES : 2 * LANES]
        block[8 * f + 4 : 8 * f + 8, :] = cols[f][4:8, LANES : 2 * LANES]
    rim = jnp.concatenate([upper, block[...].T], axis=0)
    for f, (source, target) in enumerate(((h_in, h_out), (m_in, m_out), (n_in, n_out))):
        side = pltpu.roll(rim, (LANES - 4 - 8 * f) % LANES, 1)
        top = jnp.concatenate([rows[f][4:8], source[4:8, :]], axis=0)
        bottom = jnp.concatenate([source[ROWS - 8 : ROWS - 4, :], rows[f][16:20]], axis=0)
        for t, (at, mine) in enumerate(((0, lane < 4), (COLS - LANES, lane >= LANES - 4))):
            part = slice(at, at + LANES)
            value = jnp.concatenate(
                [top[:, part], source[8 : ROWS - 8, part], bottom[:, part]], axis=0
            )
            sides[f, t] = jnp.where(mine, side, value)
            copies.append(
                pltpu.make_async_copy(sides.at[f, t], target.at[:, part], sems.at[1 + t, f])
            )
        for t, (at, value) in enumerate(((0, top), (ROWS - 8, bottom))):
            ends[f, t] = value[:, inner]
            copies.append(
                pltpu.make_async_copy(ends.at[f, t], target.at[at : at + 8, inner], sems.at[3 + t, f])
            )
        for copy in copies[-4:]:
            copy.start()
    for copy in copies:
        copy.wait()


def f32(*shape):
    return jax.ShapeDtypeStruct(shape, jnp.float32)


SMEM = pl.BlockSpec(memory_space=pltpu.SMEM)
VMEM = pl.BlockSpec(memory_space=pltpu.VMEM)
HBM = pl.BlockSpec(memory_space=pltpu.HBM)


def run(body, outs, in_specs, scratch, args, name, cost=None, out_spec=VMEM):
    if cost is not None:
        cost = pl.CostEstimate(flops=cost, bytes_accessed=0, transcendentals=0)
    return pl.pallas_call(
        body,
        in_specs=in_specs,
        out_specs=[out_spec] * len(outs),
        out_shape=outs,
        scratch_shapes=scratch,
        compiler_params=pltpu.CompilerParams(vmem_limit_bytes=VMEM_LIMIT),
        cost_estimate=cost,
        name=name,
    )(*args)


def shards(slip_rate, green_kernel, intersection, wet_mask, column_height, east_flow, north_flow):
    place = jnp.stack([lax.axis_index("ox"), lax.axis_index("oy")]).astype(jnp.int32)
    fields = (column_height, east_flow, north_flow, wet_mask)

    msg_a, msg_b, mid_a, mid_b, far_a, far_b, own, rim = run(
        slip_kernel,
        [f32(ROW_MSG, LANES)] * 2 + [f32(MID_MSG, LANES)] * 2 + [f32(16, LANES)] * 2
        + [f32(3, RING, LANES), f32(8, LANES)],
        [SMEM] + [HBM] * 7,
        [
            pltpu.VMEM((9, 32, UX * LANES), jnp.bfloat16),
            pltpu.SMEM((1, 9), jnp.int32),
            pltpu.VMEM((STEPS, 32), jnp.bfloat16),
            pltpu.VMEM((3, 2, 8, COLS), jnp.float32),
            pltpu.VMEM((2, 8, COLS), jnp.int32),
            pltpu.VMEM((MAIN, LANES), jnp.float32),
            pltpu.SemaphoreType.DMA((19,)),
        ],
        (place,)
        + tuple(
            pltpu.with_memory_space_constraint(x, pltpu.HBM)
            for x in (intersection, slip_rate, jnp.transpose(green_kernel, (1, 0, 2))) + fields
        ),
        "slip",
    )
    got_a = swap(msg_a, "ox", 0)
    got_b = swap(msg_b, "ox", 1)
    gotfar_a = swap(far_a, "ox", 0, 2)
    gotfar_b = swap(far_b, "ox", 1, 2)
    mid_a = swap(mid_a, "ox", 0)
    mid_b = swap(mid_b, "ox", 1)

    *near, moved = run(
        first_kernel,
        [f32(ROWS, COLS)] * 3 + [jax.ShapeDtypeStruct((ROWS, COLS), jnp.int32), f32(3, ROWS, COLS)],
        [HBM] * 4,
        [pltpu.SemaphoreType.DMA((5, 3))],
        [pltpu.with_memory_space_constraint(x, pltpu.HBM) for x in fields],
        "first",
    )
    near = tuple(near)
    msg_a, msg_b, far_a, far_b, tail1, ring, turned_own, edges = run(
        column_kernel,
        [f32(COL_MSG, LANES)] * 2 + [f32(8, LANES)] * 4 + [f32(3, 64, LANES), f32(4, 8, COLS)],
        [SMEM] + [VMEM] * 10,
        [pltpu.VMEM((TALL, LANES), jnp.float32)],
        (place, own, rim, got_a, got_b, gotfar_a, gotfar_b) + near,
        "column",
        10**10,
    )
    got_a = swap(msg_a, "oy", 0)
    got_b = swap(msg_b, "oy", 1)
    gotfar_a = swap(far_a, "oy", 0, 2)
    gotfar_b = swap(far_b, "oy", 1, 2)

    height, east, north, total = run(
        main_kernel,
        [f32(ROWS, COLS)] * 3 + [f32(MAIN, LANES)],
        [SMEM] + [VMEM] * 7,
        [
            pltpu.VMEM((2, 3, ROWS, COLS), jnp.float32),
            pltpu.VMEM((MAIN, COLS), jnp.float32),
        ],
        (place, own, mid_a, mid_b, got_a, got_b, moved, near[3]),
        "main",
        10**10,
    )
    return tuple(
        run(
            strip_kernel,
            [f32(ROWS, COLS)] * 3,
            [SMEM] + [VMEM] * 16,
            [
                pltpu.VMEM((LANES, LANES), jnp.float32),
                pltpu.VMEM((3, 2, ROWS, LANES), jnp.float32),
                pltpu.VMEM((3, 2, 8, COLS - 2 * LANES), jnp.float32),
                pltpu.SemaphoreType.DMA((5, 3)),
            ],
            (place, total, tail1, got_a, got_b, gotfar_a, gotfar_b, ring, turned_own, edges)
            + near + (height, east, north),
            "strip",
            out_spec=HBM,
        )
    )


def solution(mesh):
    return jax.shard_map(
        shards,
        mesh=mesh,
        in_specs=(
            P(None, ("ox", "oy")),
            P(("ox", "oy"), None, None),
            P(("ox", "oy"), None),
            P("ox", "oy"),
            P("ox", "oy"),
            P("ox", "oy"),
            P("ox", "oy"),
        ),
        out_specs=(P("ox", "oy"), P("ox", "oy"), P("ox", "oy")),
        check_vma=False,
    )
```

```python
import functools

import jax
import jax.numpy as jnp
from jax import lax
from jax.experimental import pallas as pl
from jax.experimental.pallas import tpu as pltpu
from jax.sharding import PartitionSpec as P

STEPS = 4
SIDE = 16
ROWS = 256
COLS = 512
LANES = 128
UX = 64
MAIN = STEPS * UX
RING = MAIN + 8
SLIVER = 2 * MAIN
EDGE = SLIVER + 16
RIM = EDGE + 64
ROW_MSG = RIM + 8
TURNED = RING
COL_MSG = RING + 48
MID_MSG = COL_MSG + 8
TALL = 3 * LANES
UNROLL = 16
VMEM_LIMIT = 24 * 1024 * 1024


def partners(axis, parity, reach):
    return [
        (i, (i + reach if (i // reach) % 2 == parity else i - reach) % SIDE)
        for i in range(SIDE)
    ]


def swap(value, axis, parity, reach=1):
    return lax.ppermute(value, axis, partners(axis, parity, reach))


def slip_kernel(
    place, cover_in, slip_in, green, h_in, m_in, n_in, w_in,
    msg_a, msg_b, mid_a, mid_b, far_a, far_b, own, rim, held, cover, slip, edge_f, edge_i, lanes, sems,
):
    def fetch(slot):
        return pltpu.make_async_copy(green.at[slot], held.at[slot], sems.at[slot])

    small = [
        pltpu.make_async_copy(slip_in, slip, sems.at[9]),
        pltpu.make_async_copy(cover_in, cover, sems.at[10]),
    ]
    edges = []
    for f, field in enumerate((h_in, m_in, n_in, w_in)):
        for t, start in enumerate((0, ROWS - 8)):
            target = edge_f.at[f, t] if f < 3 else edge_i.at[t]
            edges.append(
                pltpu.make_async_copy(field.at[start : start + 8], target, sems.at[11 + 2 * f + t])
            )
    for copy in small:
        copy.start()
    order = (0, 6, 3, 1, 7, 4, 2, 8, 5)
    for slot in order:
        fetch(slot).start()
    for copy in edges:
        copy.start()
    for copy in small:
        copy.wait()
    even = place[0] % 2 == 0
    even2 = (place[0] // 2) % 2 == 0

    rates = slip[...].astype(jnp.float32)
    rates = jnp.concatenate([rates] * 8, axis=1)
    rates = jnp.concatenate(
        [jnp.broadcast_to(rates[s : s + 1], (8, 256)) for s in range(STEPS)], axis=0
    )
    row = lax.broadcasted_iota(jnp.int32, (32, 256), 0)
    col = lax.broadcasted_iota(jnp.int32, (32, 256), 1)
    spread = jnp.where(col // 32 == row % 8, rates, 0.0).astype(jnp.bfloat16)
    lane = lax.broadcasted_iota(jnp.int32, (32, LANES), 1)

    def group(slot, g):
        right = jnp.concatenate(
            [held[slot, :, (g * 8 + p) * LANES : (g * 8 + p + 1) * LANES] for p in range(8)],
            axis=0,
        )
        value = jnp.dot(spread, right, preferred_element_type=jnp.float32)
        return value * cover[0, slot].astype(jnp.float32)

    def rims(down, up, mid):
        value = jnp.where(lane == 1, pltpu.roll(up, 1, 1), down)
        value = jnp.where(lane == LANES - 2, pltpu.roll(up, LANES - 1, 1), value)
        value = jnp.where(lane == 2, pltpu.roll(mid, 2, 1), value)
        return jnp.where(lane == LANES - 3, pltpu.roll(mid, LANES - 2, 1), value)

    for b in range(3):
        fetch(b).wait()
        fetch(6 + b).wait()
        fetch(3 + b).wait()
        to_a, to_b, base = ((msg_a, msg_b, 0), (mid_a, mid_b, 0), (msg_a, msg_b, MAIN))[b]
        for g in range(8):
            up = group(b, g)
            down = group(6 + b, g)
            mid = group(3 + b, g)
            first = jnp.where(even, down, up)
            second = jnp.where(even, up, down)
            if b == 1:
                rim_lanes = rims(down, up, mid)
            for s in range(STEPS):
                part = slice(8 * s, 8 * s + 8)
                at = s * UX + g * 8
                to_a[base + at : base + at + 8, :] = first[part]
                to_b[base + at : base + at + 8, :] = second[part]
                own[b, at : at + 8, :] = mid[part]
                if b == 1:
                    lanes[at : at + 8, :] = rim_lanes[part]
            if g == 0:
                for s in range(STEPS):
                    own[b, MAIN + s : MAIN + s + 1, :] = down[8 * s : 8 * s + 1]
                up_edge, up_mid = up, mid
            if g == 7:
                for s in range(STEPS):
                    own[b, MAIN + 4 + s : MAIN + 5 + s, :] = up[8 * s + 7 : 8 * s + 8]
                    at = b * STEPS + s
                    to_down = mid[8 * s + 7 : 8 * s + 8]
                    to_up = up_mid[8 * s : 8 * s + 1]
                    msg_a[SLIVER + at : SLIVER + at + 1, :] = jnp.where(even, to_down, to_up)
                    msg_b[SLIVER + at : SLIVER + at + 1, :] = jnp.where(even, to_up, to_down)
                    to_down = down[8 * s + 7 : 8 * s + 8]
                    to_up = up_edge[8 * s : 8 * s + 1]
                    far_a[at : at + 1, :] = jnp.where(even2, to_down, to_up)
                    far_b[at : at + 1, :] = jnp.where(even2, to_up, to_down)
    blank = jnp.zeros((4, LANES), jnp.float32)
    for ref, start in ((msg_a, SLIVER + 12), (msg_b, SLIVER + 12), (far_a, 12), (far_b, 12)):
        ref[start : start + 4, :] = blank
    for ref, start in ((msg_a, RIM + 4), (msg_b, RIM + 4), (rim, 4)):
        ref[start : start + 4, :] = blank
    for ref in (mid_a, mid_b):
        ref[MAIN:MID_MSG, :] = jnp.zeros((MID_MSG - MAIN, LANES), jnp.float32)
    for k in range(2):
        turned = lanes[k * LANES : (k + 1) * LANES, :].T
        to_down = jnp.concatenate([turned[0:1], turned[127:128]], axis=0)
        to_up = jnp.concatenate([turned[1:2], turned[126:127]], axis=0)
        at = RIM + 2 * k
        msg_a[at : at + 2, :] = jnp.where(even, to_down, to_up)
        msg_b[at : at + 2, :] = jnp.where(even, to_up, to_down)
        rim[2 * k : 2 * k + 1, :] = turned[2:3]
        rim[2 * k + 1 : 2 * k + 2, :] = turned[125:126]

    for copy in edges:
        copy.wait()
    for f in range(4):
        top, bottom = (edge_f[f, 0], edge_f[f, 1]) if f < 3 else (edge_i[0], edge_i[1])
        to_up = top[0:4].astype(jnp.float32)
        to_down = bottom[4:8].astype(jnp.float32)
        first = jnp.where(even, to_down, to_up)
        second = jnp.where(even, to_up, to_down)
        for k in range(4):
            at = EDGE + (f * 4 + k) * 4
            msg_a[at : at + 4, :] = first[:, k * LANES : (k + 1) * LANES]
            msg_b[at : at + 4, :] = second[:, k * LANES : (k + 1) * LANES]


def tuck(packed, lane, block, source, target, count):
    moved = pltpu.roll(block, (target - source) % LANES, 1) if target != source else block
    return jnp.where((lane >= target) & (lane < target + count), moved, packed)


def column_kernel(
    place, own, rim, got_a, got_b, gotfar_a, gotfar_b, rim_state,
    msg_a, msg_b, far_a, far_b, tail1, ring, turned_own, edges, lanes,
):
    i, j = place[0], place[1]
    even = i % 2 == 0
    even2 = (i // 2) % 2 == 0
    above_ok, below_ok = i > 0, i < SIDE - 1
    above2_ok, below2_ok = i > 1, i < SIDE - 2
    even_j = j % 2 == 0
    even2_j = (j // 2) % 2 == 0

    def from_above(rows):
        return jnp.where(even, got_b[rows, :], got_a[rows, :])

    def from_below(rows):
        return jnp.where(even, got_a[rows, :], got_b[rows, :])

    tails = []
    for b in range(3):
        rows = slice(SLIVER + 4 * b, SLIVER + 4 * b + 4)
        far = slice(4 * b, 4 * b + 4)
        above = jnp.where(above_ok, from_above(rows), 0.0)
        above = above + jnp.where(
            above2_ok, jnp.where(even2, gotfar_b[far, :], gotfar_a[far, :]), 0.0
        )
        below = jnp.where(below_ok, from_below(rows), 0.0)
        below = below + jnp.where(
            below2_ok, jnp.where(even2, gotfar_a[far, :], gotfar_b[far, :]), 0.0
        )
        tails.append(own[b, MAIN:RING, :] + jnp.concatenate([below, above], axis=0))
    tail1[...] = tails[1]

    sums = []
    for b, base in ((0, 0), (2, MAIN)):
        rows = slice(base, base + MAIN)
        main = own[b, 0:MAIN, :]
        main = main + jnp.where(above_ok, from_above(rows), 0.0)
        main = main + jnp.where(below_ok, from_below(rows), 0.0)
        sums.append(main)
    left_sum, right_sum = sums
    msg_a[0:MAIN, :] = jnp.where(even_j, right_sum, left_sum)
    msg_b[0:MAIN, :] = jnp.where(even_j, left_sum, right_sum)
    msg_a[MAIN:RING, :] = jnp.where(even_j, tails[2], tails[0])
    msg_b[MAIN:RING, :] = jnp.where(even_j, tails[0], tails[2])

    for f in range(4):
        for k in range(4):
            rows = slice(EDGE + (f * 4 + k) * 4, EDGE + (f * 4 + k) * 4 + 4)
            edges[f, :, k * LANES : (k + 1) * LANES] = jnp.concatenate(
                [from_below(rows), from_above(rows)], axis=0
            )

    lane = lax.broadcasted_iota(jnp.int32, (ROWS, LANES), 1)
    packed = rim_state[...]
    lane8 = lax.broadcasted_iota(jnp.int32, (8, LANES), 1)
    packed8 = jnp.zeros((8, LANES), jnp.float32)
    for f in range(4):
        packed8 = tuck(packed8, lane8, edges[f, :, COLS - LANES : COLS], LANES - 8, 8 * f, 8)
        packed8 = tuck(packed8, lane8, edges[f, :, 0:LANES], 0, 32 + 8 * f, 8)
    spots = ((2, LANES - 1, 64), (0, 0, 65), (0, LANES - 1, 66), (2, 0, 67))
    for b, source, target in spots:
        packed = tuck(packed, lane, sums[b // 2], source, target, 1)
        packed8 = tuck(packed8, lane8, tails[b], source, target, 1)
    packed8 = tuck(packed8, lane8, tails[1], 0, 68, 1)
    packed8 = tuck(packed8, lane8, tails[1], LANES - 1, 69, 1)
    lanes[0:ROWS, :] = packed
    lanes[ROWS : ROWS + 4, :] = packed8[0:4]
    lanes[ROWS + 4 : TALL - 4, :] = jnp.zeros((TALL - ROWS - 8, LANES), jnp.float32)
    lanes[TALL - 4 : TALL, :] = packed8[4:8]

    zero8 = jnp.zeros((8, LANES), jnp.float32)
    far_a[...] = zero8
    far_b[...] = zero8
    ring[...] = zero8
    for k in range(3):
        turned = lanes[k * LANES : (k + 1) * LANES, :].T
        turned_own[k] = turned[0:64]
        if k < 2:
            rims = []
            for side in range(2):
                row = slice(RIM + 2 * k + side, RIM + 2 * k + side + 1)
                value = rim[2 * k + side : 2 * k + side + 1, :]
                value = value + jnp.where(above_ok, from_above(row), 0.0)
                rims.append(value + jnp.where(below_ok, from_below(row), 0.0))
        else:
            rims = [turned[68:69], turned[69:70]]
        to_right = [turned[8 * f + 4 : 8 * f + 8] for f in range(3)] + [rims[1], turned[29:32]]
        to_left = [turned[32 + 8 * f : 36 + 8 * f] for f in range(3)] + [turned[56:59], rims[0]]
        to_right = jnp.concatenate(to_right, axis=0)
        to_left = jnp.concatenate(to_left, axis=0)
        at = TURNED + 16 * k
        msg_a[at : at + 16, :] = jnp.where(even_j, to_right, to_left)
        msg_b[at : at + 16, :] = jnp.where(even_j, to_left, to_right)
        far_a[k : k + 1, :] = jnp.where(even2_j, turned[64:65], turned[65:66])
        far_b[k : k + 1, :] = jnp.where(even2_j, turned[65:66], turned[64:65])
        ring[k : k + 1, :] = turned[66:67]
        ring[4 + k : 5 + k, :] = turned[67:68]


def spread_matrix():
    coarse = lax.broadcasted_iota(jnp.int32, (LANES, COLS), 0)
    fine = lax.broadcasted_iota(jnp.int32, (LANES, COLS), 1)
    return jnp.where(fine // 4 == coarse, 1.0, 0.0).astype(jnp.bfloat16)


def widen(value, spread):
    part = value.astype(jnp.bfloat16)
    rest = (value - part.astype(jnp.float32)).astype(jnp.bfloat16)
    dot = functools.partial(jnp.dot, preferred_element_type=jnp.float32)
    return dot(part, spread) + dot(rest, spread)


def fluxes(height, east, north):
    inverse = 1.0 / height
    v = north * inverse
    pressure = 0.05 * height * height
    fm = 0.1 * east
    gn = 0.1 * north
    fmm = fm * (east * inverse) + pressure
    fmn = fm * v
    gnn = gn * v + pressure
    quarter = (0.25 * height, 0.25 * east, 0.25 * north)
    return quarter, (fm, fmm, fmn), (gn, fmn, gnn)


def interior_step(load, store, ready=None):
    sub = lax.broadcasted_iota(jnp.int32, (8, COLS), 0)
    first_row, last_row = sub == 0, sub == 7
    zeros = jnp.zeros((8, COLS), jnp.float32)

    def finish(at, partial, ahead, beyond):
        store(at, [p + jnp.where(last_row, b, a) for p, a, b in zip(partial, ahead, beyond)])

    def body(c, carry):
        partial, above, before = carry
        at = pl.multiple_of(c * 8, 8)
        quarter, east_flux, north_flux = fluxes(*load(at))
        below = [pltpu.roll(q + x, 1, 0) for q, x in zip(quarter, east_flux)]
        ahead = [pltpu.roll(q - x, 7, 0) for q, x in zip(quarter, east_flux)]
        new_partial = [
            pltpu.roll(q - g, COLS - 1, 1)
            + pltpu.roll(q + g, 1, 1)
            + jnp.where(first_row, a, b)
            for q, g, a, b in zip(quarter, north_flux, above, below)
        ]
        finish(pl.multiple_of(jnp.maximum(c - 1, 0) * 8, 8), partial, before, ahead)
        return new_partial, below, ahead

    carry = ([zeros] * 3, [zeros] * 3, [zeros] * 3)
    if ready is None:
        carry = lax.fori_loop(0, ROWS // 8, body, carry, unroll=UNROLL)
    else:
        for q in range(4):
            ready(q)
            carry = lax.fori_loop(q * 8, q * 8 + 8, body, carry, unroll=8)
    finish(ROWS - 8, carry[0], carry[2], carry[2])


def first_kernel(h_in, m_in, n_in, w_in, h_near, m_near, n_near, w_near, moved, rim_state, sems):
    part = ROWS // 4
    pairs = ((h_in, h_near), (m_in, m_near), (n_in, n_near))

    def fetch(pair, q, sem):
        rows = slice(q * part, q * part + part)
        return pltpu.make_async_copy(pair[0].at[rows], pair[1].at[rows], sem)

    copies = [[fetch(pair, q, sems.at[q, f]) for f, pair in enumerate(pairs)] for q in range(4)]
    mask = pltpu.make_async_copy(w_in, w_near, sems.at[4, 0])
    for q in range(4):
        for copy in copies[q]:
            copy.start()
    mask.start()

    def load(at):
        return [ref[pl.ds(at, 8), :] for ref in (h_near, m_near, n_near)]

    def store(at, values):
        for f in range(3):
            moved[f, pl.ds(at, 8), :] = values[f]

    def ready(q):
        for copy in copies[q]:
            copy.wait()

    interior_step(load, store, ready)
    mask.wait()
    lane = lax.broadcasted_iota(jnp.int32, (ROWS, LANES), 1)
    packed = jnp.zeros((ROWS, LANES), jnp.float32)
    for f, field in enumerate((h_near, m_near, n_near, w_near)):
        right = field[:, COLS - LANES : COLS].astype(jnp.float32)
        packed = tuck(packed, lane, right, LANES - 8, 8 * f, 8)
        left = field[:, 0:LANES].astype(jnp.float32)
        packed = tuck(packed, lane, left, 0, 32 + 8 * f, 8)
    rim_state[...] = packed


def main_kernel(
    place, own, mid_a, mid_b, got_a, got_b, moved, w_in,
    h_out, m_out, n_out, total, state, lift,
):
    i, j = place[0], place[1]
    even = i % 2 == 0
    even_j = j % 2 == 0
    rows = slice(0, MAIN)
    value = own[1, rows, :]
    value = value + jnp.where(i > 0, jnp.where(even, mid_b[rows, :], mid_a[rows, :]), 0.0)
    value = value + jnp.where(i < SIDE - 1, jnp.where(even, mid_a[rows, :], mid_b[rows, :]), 0.0)
    value = value + jnp.where(j > 0, jnp.where(even_j, got_b[rows, :], got_a[rows, :]), 0.0)
    value = value + jnp.where(
        j < SIDE - 1, jnp.where(even_j, got_a[rows, :], got_b[rows, :]), 0.0
    )
    total[...] = 0.05 * value
    lift[...] = widen(total[...], spread_matrix())
    upper_half = lax.broadcasted_iota(jnp.int32, (8, COLS), 0) < 4

    def source_and_mask(s, at, values):
        row = s * UX + at // 4
        raised = jnp.where(
            upper_half,
            jnp.broadcast_to(lift[pl.ds(row, 1), :], (8, COLS)),
            jnp.broadcast_to(lift[pl.ds(row + 1, 1), :], (8, COLS)),
        )
        mask = w_in[pl.ds(at, 8), :].astype(jnp.float32)
        return [values[0] + raised, values[1] * mask, values[2] * mask]

    for s in range(1, STEPS):

        def load(at, s=s):
            if s == 1:
                return source_and_mask(0, at, [moved[f, pl.ds(at, 8), :] for f in range(3)])
            return [state[s % 2, f, pl.ds(at, 8), :] for f in range(3)]

        def store(at, values, s=s):
            values = source_and_mask(s, at, values)
            for f in range(3):
                if s == STEPS - 1:
                    (h_out, m_out, n_out)[f][pl.ds(at, 8), :] = values[f]
                else:
                    state[(s + 1) % 2, f, pl.ds(at, 8), :] = values[f]

        interior_step(load, store)


def strip_kernel(
    place, total, tail1, got_a, got_b, gotfar_a, gotfar_b, ring, turned_own, edges,
    h_0, m_0, n_0, w_in, h_in, m_in, n_in, h_out, m_out, n_out, block, sides, ends, sems,
):
    inner = slice(LANES, COLS - LANES)
    copies = []
    for f, (source, target) in enumerate(((h_in, h_out), (m_in, m_out), (n_in, n_out))):
        rows = slice(8, ROWS - 8)
        copies.append(
            pltpu.make_async_copy(source.at[rows, inner], target.at[rows, inner], sems.at[0, f])
        )
        copies[f].start()

    i, j = place[0], place[1]
    even_j = j % 2 == 0
    even2_j = (j // 2) % 2 == 0
    spread = spread_matrix()

    def from_left(rows):
        return jnp.where(even_j, got_b[rows, :], got_a[rows, :])

    def from_right(rows):
        return jnp.where(even_j, got_a[rows, :], got_b[rows, :])

    tail = tail1[...] + jnp.where(j > 0, from_left(slice(MAIN, RING)), 0.0)
    tail = 0.05 * (tail + jnp.where(j < SIDE - 1, from_right(slice(MAIN, RING)), 0.0))

    def six(values):
        return jnp.concatenate([jnp.broadcast_to(v, (4, v.shape[1])) for v in values], axis=0)

    coarse = []
    for s in range(STEPS):
        at = s * UX
        coarse += [
            tail[4 + s : 5 + s], total[at : at + 2, :], total[at + UX - 2 : at + UX, :], tail[s : s + 1],
        ]
    fine = widen(jnp.concatenate(coarse, axis=0), spread)
    row_lift = [
        six([fine[6 * s + r : 6 * s + r + 1] for r in range(6)]) for s in range(STEPS)
    ]
    row_state = []
    for f, field in enumerate((h_0, m_0, n_0, w_in)):
        row_state.append(
            jnp.concatenate(
                [
                    edges[f, 4:8, :],
                    field[0:8, :].astype(jnp.float32),
                    field[ROWS - 8 : ROWS, :].astype(jnp.float32),
                    edges[f, 0:4, :],
                ],
                axis=0,
            )
        )

    parts = [[], [], [], []]
    ups = []
    for k in range(3):
        at = TURNED + 16 * k
        left, right = from_left(slice(at, at + 16)), from_right(slice(at, at + 16))
        for f in range(4):
            parts[f].append(
                jnp.concatenate(
                    [
                        left[4 * f : 4 * f + 4],
                        turned_own[k, 32 + 8 * f : 40 + 8 * f, :],
                        turned_own[k, 8 * f : 8 * f + 8, :],
                        right[4 * f : 4 * f + 4],
                    ],
                    axis=0,
                )
            )
        far_left = jnp.where(even2_j, gotfar_b[k : k + 1, :], gotfar_a[k : k + 1, :])
        far_right = jnp.where(even2_j, gotfar_a[k : k + 1, :], gotfar_b[k : k + 1, :])
        ring_left = ring[k : k + 1, :] + left[12:13] + jnp.where(j > 1, far_left, 0.0)
        ring_right = ring[4 + k : 5 + k, :] + right[15:16]
        ring_right = ring_right + jnp.where(j < SIDE - 2, far_right, 0.0)
        if k < 2:
            turned = total[k * LANES : (k + 1) * LANES, :].T
        else:
            block[...] = jnp.zeros((LANES, LANES), jnp.float32)
            block[0:4, :] = tail[0:4]
            block[LANES - 4 : LANES, :] = tail[4:8]
            turned = block[...].T
        ups.append(
            jnp.concatenate(
                [0.05 * ring_left, turned[0:2], turned[126:128], 0.05 * ring_right, turned[0:2]],
                axis=0,
            )
        )
    col_state = [jnp.concatenate(p, axis=1) for p in parts]
    lane = lax.broadcasted_iota(jnp.int32, (8, LANES), 1)
    col_lift = []
    for s in range(STEPS):
        if s % 2 == 0:
            wide = widen(ups[s // 2], spread)
        own_rows = wide[:, 256 * (s % 2) : 256 * (s % 2) + 256]
        beside = jnp.where(
            lane < 4,
            jnp.broadcast_to(ups[2][:, s : s + 1], (8, LANES)),
            jnp.broadcast_to(ups[2][:, LANES - 4 + s : LANES - 3 + s], (8, LANES)),
        )
        both = jnp.concatenate([own_rows, beside], axis=1)
        col_lift.append(six([both[r : r + 1] for r in range(6)]))

    def advance(state, lift, wet, x_axis, ends):
        n_sub, n_lane = state[0].shape
        sub = lax.broadcasted_iota(jnp.int32, (n_sub, n_lane), 0)
        lanes = lax.broadcasted_iota(jnp.int32, (n_sub, n_lane), 1)
        fixed = []
        for value in state:
            value = jnp.where((sub == 3) & ends[0], pltpu.roll(value, n_sub - 1, 0), value)
            value = jnp.where((sub == 20) & ends[1], pltpu.roll(value, 1, 0), value)
            if len(ends) == 4:
                blocks = [value[:, k * LANES : (k + 1) * LANES] for k in range(3)]
                last = lanes[:, 0:LANES] == LANES - 1
                blocks[2] = jnp.where(last & ends[2], pltpu.roll(blocks[0], LANES - 1, 1), blocks[2])
                initial = lanes[:, 0:LANES] == 0
                blocks[2] = jnp.where(initial & ends[3], pltpu.roll(blocks[1], 1, 1), blocks[2])
                value = jnp.concatenate(blocks, axis=1)
            fixed.append(value)
        quarter, east_flux, north_flux = fluxes(*fixed)
        along_sub, along_lane = (east_flux, north_flux) if x_axis == 0 else (north_flux, east_flux)
        out = [
            pltpu.roll(q - a, n_sub - 1, 0)
            + pltpu.roll(q + a, 1, 0)
            + pltpu.roll(q - l, n_lane - 1, 1)
            + pltpu.roll(q + l, 1, 1)
            for q, a, l in zip(quarter, along_sub, along_lane)
        ]
        return [out[0] + lift, out[1] * wet, out[2] * wet]

    row_ends = (i == 0, i == SIDE - 1)
    col_ends = (j == 0, j == SIDE - 1) + row_ends
    rows, cols = row_state[:3], col_state[:3]
    for s in range(STEPS):
        rows = advance(rows, row_lift[s], row_state[3], 0, row_ends)
        cols = advance(cols, col_lift[s], col_state[3], 1, col_ends)

    lane = lax.broadcasted_iota(jnp.int32, (ROWS, LANES), 1)
    for f in range(3):
        block[8 * f : 8 * f + 4, :] = cols[f][16:20, 0:LANES]
        block[8 * f + 4 : 8 * f + 8, :] = cols[f][4:8, 0:LANES]
    upper = block[...].T
    for f in range(3):
        block[8 * f : 8 * f + 4, :] = cols[f][16:20, LANES : 2 * LANES]
        block[8 * f + 4 : 8 * f + 8, :] = cols[f][4:8, LANES : 2 * LANES]
    rim = jnp.concatenate([upper, block[...].T], axis=0)
    for f, (source, target) in enumerate(((h_in, h_out), (m_in, m_out), (n_in, n_out))):
        side = pltpu.roll(rim, (LANES - 4 - 8 * f) % LANES, 1)
        top = jnp.concatenate([rows[f][4:8], source[4:8, :]], axis=0)
        bottom = jnp.concatenate([source[ROWS - 8 : ROWS - 4, :], rows[f][16:20]], axis=0)
        for t, (at, mine) in enumerate(((0, lane < 4), (COLS - LANES, lane >= LANES - 4))):
            part = slice(at, at + LANES)
            value = jnp.concatenate(
                [top[:, part], source[8 : ROWS - 8, part], bottom[:, part]], axis=0
            )
            sides[f, t] = jnp.where(mine, side, value)
            copies.append(
                pltpu.make_async_copy(sides.at[f, t], target.at[:, part], sems.at[1 + t, f])
            )
        for t, (at, value) in enumerate(((0, top), (ROWS - 8, bottom))):
            ends[f, t] = value[:, inner]
            copies.append(
                pltpu.make_async_copy(ends.at[f, t], target.at[at : at + 8, inner], sems.at[3 + t, f])
            )
        for copy in copies[-4:]:
            copy.start()
    for copy in copies:
        copy.wait()


def f32(*shape):
    return jax.ShapeDtypeStruct(shape, jnp.float32)


SMEM = pl.BlockSpec(memory_space=pltpu.SMEM)
VMEM = pl.BlockSpec(memory_space=pltpu.VMEM)
HBM = pl.BlockSpec(memory_space=pltpu.HBM)


def run(body, outs, in_specs, scratch, args, name, cost=None, out_spec=VMEM):
    if cost is not None:
        cost = pl.CostEstimate(flops=cost, bytes_accessed=0, transcendentals=0)
    return pl.pallas_call(
        body,
        in_specs=in_specs,
        out_specs=[out_spec] * len(outs),
        out_shape=outs,
        scratch_shapes=scratch,
        compiler_params=pltpu.CompilerParams(vmem_limit_bytes=VMEM_LIMIT),
        cost_estimate=cost,
        name=name,
    )(*args)


def shards(slip_rate, green_kernel, intersection, wet_mask, column_height, east_flow, north_flow):
    place = jnp.stack([lax.axis_index("ox"), lax.axis_index("oy")]).astype(jnp.int32)
    fields = (column_height, east_flow, north_flow, wet_mask)

    msg_a, msg_b, mid_a, mid_b, far_a, far_b, own, rim = run(
        slip_kernel,
        [f32(ROW_MSG, LANES)] * 2 + [f32(MID_MSG, LANES)] * 2 + [f32(16, LANES)] * 2
        + [f32(3, RING, LANES), f32(8, LANES)],
        [SMEM] + [HBM] * 7,
        [
            pltpu.VMEM((9, 32, UX * LANES), jnp.bfloat16),
            pltpu.SMEM((1, 9), jnp.int32),
            pltpu.VMEM((STEPS, 32), jnp.bfloat16),
            pltpu.VMEM((3, 2, 8, COLS), jnp.float32),
            pltpu.VMEM((2, 8, COLS), jnp.int32),
            pltpu.VMEM((MAIN, LANES), jnp.float32),
            pltpu.SemaphoreType.DMA((19,)),
        ],
        (place,)
        + tuple(
            pltpu.with_memory_space_constraint(x, pltpu.HBM)
            for x in (intersection, slip_rate, jnp.transpose(green_kernel, (1, 0, 2))) + fields
        ),
        "slip",
    )
    got_a = swap(msg_a, "ox", 0)
    got_b = swap(msg_b, "ox", 1)
    gotfar_a = swap(far_a, "ox", 0, 2)
    gotfar_b = swap(far_b, "ox", 1, 2)
    mid_a = swap(mid_a, "ox", 0)
    mid_b = swap(mid_b, "ox", 1)

    *near, moved, rim_state = run(
        first_kernel,
        [f32(ROWS, COLS)] * 3 + [jax.ShapeDtypeStruct((ROWS, COLS), jnp.int32), f32(3, ROWS, COLS), f32(ROWS, LANES)],
        [HBM] * 4,
        [pltpu.SemaphoreType.DMA((5, 3))],
        [pltpu.with_memory_space_constraint(x, pltpu.HBM) for x in fields],
        "first",
    )
    near = tuple(near)
    msg_a, msg_b, far_a, far_b, tail1, ring, turned_own, edges = run(
        column_kernel,
        [f32(COL_MSG, LANES)] * 2 + [f32(8, LANES)] * 4 + [f32(3, 64, LANES), f32(4, 8, COLS)],
        [SMEM] + [VMEM] * 7,
        [pltpu.VMEM((TALL, LANES), jnp.float32)],
        (place, own, rim, got_a, got_b, gotfar_a, gotfar_b, rim_state),
        "column",
        10**10,
    )
    got_a = swap(msg_a, "oy", 0)
    got_b = swap(msg_b, "oy", 1)
    gotfar_a = swap(far_a, "oy", 0, 2)
    gotfar_b = swap(far_b, "oy", 1, 2)

    height, east, north, total = run(
        main_kernel,
        [f32(ROWS, COLS)] * 3 + [f32(MAIN, LANES)],
        [SMEM] + [VMEM] * 7,
        [
            pltpu.VMEM((2, 3, ROWS, COLS), jnp.float32),
            pltpu.VMEM((MAIN, COLS), jnp.float32),
        ],
        (place, own, mid_a, mid_b, got_a, got_b, moved, near[3]),
        "main",
        10**10,
    )
    return tuple(
        run(
            strip_kernel,
            [f32(ROWS, COLS)] * 3,
            [SMEM] + [VMEM] * 16,
            [
                pltpu.VMEM((LANES, LANES), jnp.float32),
                pltpu.VMEM((3, 2, ROWS, LANES), jnp.float32),
                pltpu.VMEM((3, 2, 8, COLS - 2 * LANES), jnp.float32),
                pltpu.SemaphoreType.DMA((5, 3)),
            ],
            (place, total, tail1, got_a, got_b, gotfar_a, gotfar_b, ring, turned_own, edges)
            + near + (height, east, north),
            "strip",
            out_spec=HBM,
        )
    )


def solution(mesh):
    return jax.shard_map(
        shards,
        mesh=mesh,
        in_specs=(
            P(None, ("ox", "oy")),
            P(("ox", "oy"), None, None),
            P(("ox", "oy"), None),
            P("ox", "oy"),
            P("ox", "oy"),
            P("ox", "oy"),
            P("ox", "oy"),
        ),
        out_specs=(P("ox", "oy"), P("ox", "oy"), P("ox", "oy")),
        check_vma=False,
    )
```
